768 devices in a mesh: ctx: 192 (over z_lo, y, x, core), tp: 4 (over z_hi).
Axes of the slice: x: 4, y: 8, z: 12 (z_hi: 4, z_lo: 3; z = z_hi * 3 + z_lo), core: 2. Of those that a mesh axis runs over, the one named last changes fastest.
Arguments:
- queries: bfloat16 [6144, 2560], P(('ctx', 'tp')), may hold values from -128 to 128
- keys: bfloat16 [6144, 2560], P(('ctx', 'tp')), may hold values from -5 to 5
- vals: bfloat16 [6144, 2560], P(('ctx', 'tp')), may hold values from -24 to 24
- out_weight: bfloat16 [2560, 5120], P(None, 'tp'), may hold values from -0.25 to 0.25
- gate: float32 [5120], P('tp'), may hold values from 0.5 to 4
Outputs:
- mixed: bfloat16 [6144, 5120], P('ctx', 'tp')
The draws below stay inside these ranges and needn't reach their ends.
All inputs are finite; a program needn't handle non-finite values.
Results may differ from the reference program's by a relative error of at most 0.0057.
Values may be sent and summed in bfloat16 or wider, within the bound.
No kernel may reach another device: no remote copies, remote signals or barrier semaphores. Data moves between devices by JAX's collectives and lax.ppermute only.
A program may use at most 64 MiB of HBM per device.

```python
import math
import jax
import jax.numpy as jnp
from jax import lax

D = 5120
HEADS = 20
HEAD_DIM = 128
TOKENS = 6144


def attention_pair(key):
    query_key, key_key = jax.random.split(jax.random.fold_in(key, 23), 2)
    width = HEADS * HEAD_DIM
    query_draw = jnp.clip(jax.random.normal(query_key, (TOKENS, width), jnp.float32), -4.5, 4.5)
    key_draw = jnp.clip(jax.random.normal(key_key, (TOKENS, width), jnp.float32), -4.5, 4.5)
    return (query_draw, key_draw)


def draw_queries(key, part):
    return attention_pair(key)[0].astype(jnp.bfloat16)


def draw_keys(key, part):
    return attention_pair(key)[1].astype(jnp.bfloat16)


def block_levels(stream_key, extent, pieces, least, top_value):
    factor_of, own = 1.0, jax.random.fold_in(stream_key, 6)
    for position, blocks in pieces:
        steps = jnp.exp(jax.random.uniform(jax.random.fold_in(own, position), (blocks,), jnp.float32, least / len(pieces), top_value / len(pieces)))
        factor_of = factor_of * jnp.repeat(steps, extent[position] // blocks).reshape([-1 if axis == position else 1 for axis in range(len(extent))])
    return factor_of


def centred(key, shape, spread, most, cuts=(), kind=jnp.bfloat16):
    level = block_levels(key, shape, cuts, -0.22, 0.18) if cuts else 1.0
    drawn = jax.random.normal(key, shape, jnp.float32) * spread * level
    return jnp.minimum(jnp.maximum(drawn, -most), most).astype(kind)


def setup_inputs(seed: int = 0) -> dict:
    arg_keys = jax.random.split(jax.random.key(seed), 6)
    queries = draw_queries(jax.random.fold_in(arg_keys[5], 71), 0)
    keys = draw_keys(jax.random.fold_in(arg_keys[5], 71), 0)
    vals = centred(arg_keys[2], (TOKENS, HEADS * HEAD_DIM), 4.0, 24.0, ((0, 768),))
    out_weight = centred(arg_keys[3], (HEADS * HEAD_DIM, D), (HEADS * HEAD_DIM // 4) ** -0.5, 0.25, ((1, 4),))
    gate = jnp.clip(jnp.exp(math.log(4.0) - 2.0794415 * jax.random.uniform(arg_keys[4], (D,), jnp.float32) ** block_levels(arg_keys[4], (D,), ((0, 4),), -0.2, 0.2)), 0.5, 4.0)
    return dict(queries=queries, keys=keys, vals=vals, out_weight=out_weight, gate=gate)


def reference(queries, keys, vals, out_weight, gate):
    token_count = queries.shape[0]
    score_scale = HEAD_DIM ** -0.5

    def split_heads(matrix):
        return jnp.transpose(matrix.reshape(token_count, HEADS, HEAD_DIM), (1, 0, 2))

    def one_head(triple):
        query_head, key_head, value_head = triple
        scores = jnp.dot(query_head, key_head.T, preferred_element_type=jnp.float32) * score_scale
        highest = jnp.max(scores, axis=-1, keepdims=True)
        expd = jnp.exp(scores - highest)
        totals = jnp.sum(expd, axis=-1, keepdims=True)
        probs = expd.astype(jnp.bfloat16)
        return jnp.dot(probs, value_head, preferred_element_type=jnp.float32) / totals

    head_out = lax.map(one_head, (split_heads(queries), split_heads(keys), split_heads(vals)))
    attended = jnp.transpose(head_out, (1, 0, 2)).reshape(token_count, HEADS * HEAD_DIM).astype(jnp.bfloat16)
    product = jnp.dot(attended, out_weight, preferred_element_type=jnp.float32)
    return (product * gate[None, :]).astype(jnp.bfloat16)
```

```python
import jax
import jax.numpy as jnp
from jax import lax
from jax.experimental import pallas as pl
from jax.experimental.pallas import tpu as pltpu
from jax.sharding import Mesh, PartitionSpec as P

HEAD_DIM = 128
LOG2E = 1.4426950408889634
SCALE = HEAD_DIM ** -0.5
QUERY_AXES = ("y",)
KEY_AXES = ("zl", "x")
SUM_LANE = 8
PIECE_LANES = 16


def split_pieces(stats):
    high = stats.astype(jnp.bfloat16).astype(jnp.float32)
    rest = stats - high
    middle = rest.astype(jnp.bfloat16).astype(jnp.float32)
    low = rest - middle
    lane = lax.broadcasted_iota(jnp.int32, stats.shape, 1)
    spread = jnp.where(
        lane < PIECE_LANES,
        high,
        jnp.where(
            lane < 2 * PIECE_LANES,
            pltpu.roll(middle, PIECE_LANES, 1),
            pltpu.roll(low, 2 * PIECE_LANES, 1),
        ),
    )
    return spread.astype(jnp.bfloat16)


def attend_kernel(q_ref, own_ref, other_ref, out_ref):
    groups, tokens, width = q_ref.shape
    heads = width // HEAD_DIM
    rows = groups * tokens
    lane = lax.broadcasted_iota(jnp.int32, (rows, HEAD_DIM), 1)
    stats = jnp.zeros((rows, HEAD_DIM), jnp.float32)
    for head in range(heads):
        columns = pl.ds(head * HEAD_DIM, HEAD_DIM)
        query = q_ref[:, :, columns].reshape(rows, HEAD_DIM)
        scores, values = [], []
        for ref in (own_ref, other_ref):
            half = ref.shape[1] // 2
            key = ref[:, :half, columns].reshape(ref.shape[0] * half, HEAD_DIM)
            values.append(ref[:, half:, columns].reshape(ref.shape[0] * half, HEAD_DIM))
            scores.append(
                lax.dot_general(
                    query, key, (((1,), (1,)), ((), ())), preferred_element_type=jnp.float32
                )
            )
        highest = jnp.maximum(
            jnp.max(scores[0], axis=1, keepdims=True), jnp.max(scores[1], axis=1, keepdims=True)
        )
        total = jnp.zeros((rows, 1), jnp.float32)
        summed = jnp.zeros((rows, HEAD_DIM), jnp.float32)
        for score, value in zip(scores, values):
            expd = jnp.exp2((score - highest) * (SCALE * LOG2E))
            total += jnp.sum(expd, axis=1, keepdims=True)
            summed += jnp.dot(
                expd.astype(jnp.bfloat16), value, preferred_element_type=jnp.float32
            )
        out_ref[:, :, columns] = summed.astype(jnp.bfloat16).reshape(groups, tokens, HEAD_DIM)
        stats = jnp.where(lane == head, highest, stats)
        stats = jnp.where(lane == SUM_LANE + head, total, stats)
    out_ref[:, :, pl.ds(width, HEAD_DIM)] = split_pieces(stats).reshape(groups, tokens, HEAD_DIM)


def combine_kernel(part_ref, out_ref):
    groups, tokens, width = part_ref.shape
    width = width - HEAD_DIM
    heads = width // HEAD_DIM
    pieces = part_ref[:, :, pl.ds(width, HEAD_DIM)].astype(jnp.float32)
    pieces = pieces.reshape(groups * tokens, HEAD_DIM)
    stats = (
        pieces
        + pltpu.roll(pieces, HEAD_DIM - PIECE_LANES, 1)
        + pltpu.roll(pieces, HEAD_DIM - 2 * PIECE_LANES, 1)
    )
    maxima = stats.reshape(groups, tokens, HEAD_DIM)
    sums = pltpu.roll(stats, HEAD_DIM - SUM_LANE, 1).reshape(groups, tokens, HEAD_DIM)
    highest = jnp.max(maxima, axis=0, keepdims=True)
    weight = jnp.exp2((maxima - highest) * (SCALE * LOG2E))
    total = jnp.sum(weight * sums, axis=0)
    for head in range(heads):
        columns = pl.ds(head * HEAD_DIM, HEAD_DIM)
        part = part_ref[:, :, columns].astype(jnp.float32)
        summed = jnp.sum(part * weight[:, :, head : head + 1], axis=0)
        out_ref[:, columns] = (summed / total[:, head : head + 1]).astype(jnp.bfloat16)


def spread_to(block, count):
    return jnp.broadcast_to(block[None], (count, *block.shape))


def on_device(queries, keys, vals, out_weight, gate):
    parts = lax.axis_size("tp")
    rows, width = queries.shape
    head_width = width // parts
    stacked = jnp.stack([queries, keys, vals], axis=0)
    stacked = stacked.reshape(3, rows, parts, head_width).transpose(2, 0, 1, 3)
    stacked = stacked.reshape(parts, 3 * rows, head_width)
    local = lax.all_to_all(stacked, "tp", split_axis=0, concat_axis=0, tiled=True)
    local = local.reshape(parts, 3, rows, head_width).transpose(1, 0, 2, 3)
    tokens = parts * rows
    local = local.reshape(3 * tokens, head_width)
    key_value = lax.all_to_all(
        spread_to(local[tokens:], lax.axis_size(KEY_AXES)),
        KEY_AXES, split_axis=0, concat_axis=0, tiled=True,
    )
    other = lax.ppermute(key_value, "c", [(0, 1), (1, 0)])
    group = lax.all_to_all(
        spread_to(local[:tokens], lax.axis_size(QUERY_AXES)),
        QUERY_AXES, split_axis=0, concat_axis=0, tiled=True,
    )
    partial = pl.pallas_call(
        attend_kernel,
        out_shape=jax.ShapeDtypeStruct((*group.shape[:2], head_width + HEAD_DIM), jnp.bfloat16),
        name="attend",
    )(group, key_value, other)
    partial = lax.all_to_all(partial, QUERY_AXES, split_axis=0, concat_axis=0, tiled=True)
    attended = pl.pallas_call(
        combine_kernel,
        out_shape=jax.ShapeDtypeStruct((tokens, head_width), jnp.bfloat16),
        name="combine",
    )(partial)
    product = jnp.dot(
        lax.all_gather(attended, "tp", axis=1, tiled=True),
        out_weight,
        preferred_element_type=jnp.float32,
    )
    return (product * gate[None, :]).astype(jnp.bfloat16)


def solution(mesh):
    ctx = ("zl", "y", "x", "c")
    fine = Mesh(mesh.devices.reshape(3, 8, 4, 2, 4), (*ctx, "tp"))
    return jax.shard_map(
        on_device,
        mesh=fine,
        in_specs=(
            P((*ctx, "tp"), None),
            P((*ctx, "tp"), None),
            P((*ctx, "tp"), None),
            P(None, "tp"),
            P("tp"),
        ),
        out_specs=P(ctx, "tp"),
        check_vma=False,
    )
```

```python
import jax
import jax.numpy as jnp
from jax import lax
from jax.experimental import pallas as pl
from jax.experimental.pallas import tpu as pltpu
from jax.sharding import Mesh, PartitionSpec as P

HEAD_DIM = 128
LOG2E = 1.4426950408889634
SCALE = HEAD_DIM ** -0.5
QUERY_AXES = ("y",)
KEY_AXES = ("zl", "x")
SUM_LANE = 8
PIECE_LANES = 16
KERNEL_VMEM = 16 * 1024 * 1024


def split_pieces(stats):
    high = stats.astype(jnp.bfloat16).astype(jnp.float32)
    rest = stats - high
    middle = rest.astype(jnp.bfloat16).astype(jnp.float32)
    low = rest - middle
    lane = lax.broadcasted_iota(jnp.int32, stats.shape, 1)
    spread = jnp.where(
        lane < PIECE_LANES,
        high,
        jnp.where(
            lane < 2 * PIECE_LANES,
            pltpu.roll(middle, PIECE_LANES, 1),
            pltpu.roll(low, 2 * PIECE_LANES, 1),
        ),
    )
    return spread.astype(jnp.bfloat16)


def attend_kernel(q_ref, own_ref, other_ref, out_ref):
    groups, tokens, width = q_ref.shape
    heads = width // HEAD_DIM
    rows = groups * tokens
    lane = lax.broadcasted_iota(jnp.int32, (rows, HEAD_DIM), 1)
    stats = jnp.zeros((rows, HEAD_DIM), jnp.float32)
    for head in range(heads):
        columns = pl.ds(head * HEAD_DIM, HEAD_DIM)
        query = q_ref[:, :, columns].reshape(rows, HEAD_DIM)
        scores, values = [], []
        for ref in (own_ref, other_ref):
            half = ref.shape[1] // 2
            key = ref[:, :half, columns].reshape(ref.shape[0] * half, HEAD_DIM)
            values.append(ref[:, half:, columns].reshape(ref.shape[0] * half, HEAD_DIM))
            scores.append(
                lax.dot_general(
                    query, key, (((1,), (1,)), ((), ())), preferred_element_type=jnp.float32
                )
            )
        highest = jnp.maximum(
            jnp.max(scores[0], axis=1, keepdims=True), jnp.max(scores[1], axis=1, keepdims=True)
        )
        total = jnp.zeros((rows, 1), jnp.float32)
        summed = jnp.zeros((rows, HEAD_DIM), jnp.float32)
        for score, value in zip(scores, values):
            expd = jnp.exp2((score - highest) * (SCALE * LOG2E))
            total += jnp.sum(expd, axis=1, keepdims=True)
            summed += jnp.dot(
                expd.astype(jnp.bfloat16), value, preferred_element_type=jnp.float32
            )
        out_ref[:, :, columns] = summed.astype(jnp.bfloat16).reshape(groups, tokens, HEAD_DIM)
        stats = jnp.where(lane == head, highest, stats)
        stats = jnp.where(lane == SUM_LANE + head, total, stats)
    out_ref[:, :, pl.ds(width, HEAD_DIM)] = split_pieces(stats).reshape(groups, tokens, HEAD_DIM)


def combine_kernel(part_ref, out_ref):
    groups, tokens, width = part_ref.shape
    width = width - HEAD_DIM
    heads = width // HEAD_DIM
    pieces = part_ref[:, :, pl.ds(width, HEAD_DIM)].astype(jnp.float32)
    pieces = pieces.reshape(groups * tokens, HEAD_DIM)
    stats = (
        pieces
        + pltpu.roll(pieces, HEAD_DIM - PIECE_LANES, 1)
        + pltpu.roll(pieces, HEAD_DIM - 2 * PIECE_LANES, 1)
    )
    maxima = stats.reshape(groups, tokens, HEAD_DIM)
    sums = pltpu.roll(stats, HEAD_DIM - SUM_LANE, 1).reshape(groups, tokens, HEAD_DIM)
    highest = jnp.max(maxima, axis=0, keepdims=True)
    weight = jnp.exp2((maxima - highest) * (SCALE * LOG2E))
    total = jnp.sum(weight * sums, axis=0)
    for head in range(heads):
        columns = pl.ds(head * HEAD_DIM, HEAD_DIM)
        part = part_ref[:, :, columns].astype(jnp.float32)
        summed = jnp.sum(part * weight[:, :, head : head + 1], axis=0)
        out_ref[:, columns] = (summed / total[:, head : head + 1]).astype(jnp.bfloat16)


def spread_to(block, count):
    return jnp.broadcast_to(block[None], (count, *block.shape))


def on_device(queries, keys, vals, out_weight, gate):
    parts = lax.axis_size("tp")
    rows, width = queries.shape
    head_width = width // parts
    stacked = jnp.stack([queries, keys, vals], axis=0)
    stacked = stacked.reshape(3, rows, parts, head_width).transpose(2, 0, 1, 3)
    stacked = stacked.reshape(parts, 3 * rows, head_width)
    local = lax.all_to_all(stacked, "tp", split_axis=0, concat_axis=0, tiled=True)
    local = local.reshape(parts, 3, rows, head_width).transpose(1, 0, 2, 3)
    tokens = parts * rows
    local = local.reshape(3 * tokens, head_width)
    key_value = lax.all_to_all(
        spread_to(local[tokens:], lax.axis_size(KEY_AXES)),
        KEY_AXES, split_axis=0, concat_axis=0, tiled=True,
    )
    group = lax.all_gather(local[:tokens], QUERY_AXES, axis=0, tiled=False)
    key_value, group = lax.optimization_barrier((key_value, group))
    other = lax.ppermute(key_value, "c", [(0, 1), (1, 0)])
    partial = pl.pallas_call(
        attend_kernel,
        out_shape=jax.ShapeDtypeStruct((*group.shape[:2], head_width + HEAD_DIM), jnp.bfloat16),
        in_specs=[pl.BlockSpec(memory_space=pltpu.VMEM)] * 3,
        out_specs=pl.BlockSpec(memory_space=pltpu.VMEM),
        compiler_params=pltpu.CompilerParams(vmem_limit_bytes=KERNEL_VMEM),
        name="attend",
    )(group, key_value, other)
    partial = lax.all_to_all(partial, QUERY_AXES, split_axis=0, concat_axis=0, tiled=True)
    attended = pl.pallas_call(
        combine_kernel,
        out_shape=jax.ShapeDtypeStruct((tokens, head_width), jnp.bfloat16),
        in_specs=[pl.BlockSpec(memory_space=pltpu.VMEM)],
        out_specs=pl.BlockSpec(memory_space=pltpu.VMEM),
        compiler_params=pltpu.CompilerParams(vmem_limit_bytes=KERNEL_VMEM),
        name="combine",
    )(partial)
    product = jnp.dot(
        lax.all_gather(attended, "tp", axis=1, tiled=True),
        out_weight,
        preferred_element_type=jnp.float32,
    )
    return (product * gate[None, :]).astype(jnp.bfloat16)


def solution(mesh):
    ctx = ("zl", "y", "x", "c")
    fine = Mesh(mesh.devices.reshape(3, 8, 4, 2, 4), (*ctx, "tp"))
    return jax.shard_map(
        on_device,
        mesh=fine,
        in_specs=(
            P((*ctx, "tp"), None),
            P((*ctx, "tp"), None),
            P((*ctx, "tp"), None),
            P(None, "tp"),
            P("tp"),
        ),
        out_specs=P(ctx, "tp"),
        check_vma=False,
    )
```

```python
import jax
import jax.numpy as jnp
from jax import lax
from jax.experimental import pallas as pl
from jax.experimental.pallas import tpu as pltpu
from jax.sharding import Mesh, PartitionSpec as P

HEAD_DIM = 128
LOG2E = 1.4426950408889634
SCALE = HEAD_DIM ** -0.5
QUERY_AXES = ("x", "zl")
KEY_AXES = ("y",)
SUM_LANE = 8
PIECE_LANES = 16
PART_PIECES = 2
MIX_VMEM = 59 * 1024 * 1024
KERNEL_VMEM = 16 * 1024 * 1024


def split_pieces(stats):
    high = stats.astype(jnp.bfloat16).astype(jnp.float32)
    rest = stats - high
    middle = rest.astype(jnp.bfloat16).astype(jnp.float32)
    low = rest - middle
    lane = lax.broadcasted_iota(jnp.int32, stats.shape, 1)
    spread = jnp.where(
        lane < PIECE_LANES,
        high,
        jnp.where(
            lane < 2 * PIECE_LANES,
            pltpu.roll(middle, PIECE_LANES, 1),
            pltpu.roll(low, 2 * PIECE_LANES, 1),
        ),
    )
    return spread.astype(jnp.bfloat16)


def attend_kernel(q_ref, own_ref, other_ref, out_ref):
    groups, tokens, width = q_ref.shape
    heads = width // HEAD_DIM
    rows = groups * tokens
    lane = lax.broadcasted_iota(jnp.int32, (rows, HEAD_DIM), 1)
    stats = jnp.zeros((rows, HEAD_DIM), jnp.float32)
    for head in range(heads):
        columns = pl.ds(head * HEAD_DIM, HEAD_DIM)
        query = q_ref[:, :, columns].reshape(rows, HEAD_DIM)
        scores, values = [], []
        for ref in (own_ref, other_ref):
            half = ref.shape[1] // 2
            key = ref[:, :half, columns].reshape(ref.shape[0] * half, HEAD_DIM)
            values.append(ref[:, half:, columns].reshape(ref.shape[0] * half, HEAD_DIM))
            scores.append(
                lax.dot_general(
                    query, key, (((1,), (1,)), ((), ())), preferred_element_type=jnp.float32
                )
            )
        highest = jnp.maximum(
            jnp.max(scores[0], axis=1, keepdims=True), jnp.max(scores[1], axis=1, keepdims=True)
        )
        total = jnp.zeros((rows, 1), jnp.float32)
        summed = jnp.zeros((rows, HEAD_DIM), jnp.float32)
        for score, value in zip(scores, values):
            expd = jnp.exp2((score - highest) * (SCALE * LOG2E))
            total += jnp.sum(expd, axis=1, keepdims=True)
            summed += jnp.dot(
                expd.astype(jnp.bfloat16), value, preferred_element_type=jnp.float32
            )
        out_ref[:, :, columns] = summed.astype(jnp.bfloat16).reshape(groups, tokens, HEAD_DIM)
        stats = jnp.where(lane == head, highest, stats)
        stats = jnp.where(lane == SUM_LANE + head, total, stats)
    out_ref[:, :, pl.ds(width, HEAD_DIM)] = split_pieces(stats).reshape(groups, tokens, HEAD_DIM)


def combine_kernel(part_ref, out_ref):
    groups, tokens, width = part_ref.shape
    width = width - HEAD_DIM
    heads = width // HEAD_DIM
    pieces = part_ref[:, :, pl.ds(width, HEAD_DIM)].astype(jnp.float32)
    pieces = pieces.reshape(groups * tokens, HEAD_DIM)
    stats = (
        pieces
        + pltpu.roll(pieces, HEAD_DIM - PIECE_LANES, 1)
        + pltpu.roll(pieces, HEAD_DIM - 2 * PIECE_LANES, 1)
    )
    maxima = stats.reshape(groups, tokens, HEAD_DIM)
    sums = pltpu.roll(stats, HEAD_DIM - SUM_LANE, 1).reshape(groups, tokens, HEAD_DIM)
    highest = jnp.max(maxima, axis=0, keepdims=True)
    weight = jnp.exp2((maxima - highest) * (SCALE * LOG2E))
    total = jnp.sum(weight * sums, axis=0)
    for head in range(heads):
        columns = pl.ds(head * HEAD_DIM, HEAD_DIM)
        part = part_ref[:, :, columns].astype(jnp.float32)
        summed = jnp.sum(part * weight[:, :, head : head + 1], axis=0)
        out_ref[:, columns] = (summed / total[:, head : head + 1]).astype(jnp.bfloat16)


def mix_kernel(attended_ref, gate_ref, weight_ref, out_ref, held_ref, semaphores):
    parts, rows, width = attended_ref.shape
    depth = width // PART_PIECES
    copies = []
    for piece in range(parts * PART_PIECES):
        span = pl.ds(piece * depth, depth)
        copy = pltpu.make_async_copy(weight_ref.at[span], held_ref.at[span], semaphores.at[piece])
        copy.start()
        copies.append(copy)
    product = jnp.zeros(out_ref.shape, jnp.float32)
    for piece, copy in enumerate(copies):
        part, start = piece // PART_PIECES, piece % PART_PIECES * depth
        copy.wait()
        product += jnp.dot(
            attended_ref[part, :, pl.ds(start, depth)],
            held_ref[pl.ds(piece * depth, depth)],
            preferred_element_type=jnp.float32,
        )
    out_ref[...] = (product * gate_ref[...]).astype(jnp.bfloat16)


def spread_to(block, count):
    return jnp.broadcast_to(block[None], (count, *block.shape))


def on_device(queries, keys, vals, out_weight, gate):
    parts = lax.axis_size("tp")
    rows, width = queries.shape
    head_width = width // parts
    stacked = jnp.stack([queries, keys, vals], axis=0)
    stacked = stacked.reshape(3, rows, parts, head_width).transpose(2, 0, 1, 3)
    stacked = stacked.reshape(parts, 3 * rows, head_width)
    local = lax.all_to_all(stacked, "tp", split_axis=0, concat_axis=0, tiled=True)
    local = local.reshape(parts, 3, rows, head_width).transpose(1, 0, 2, 3)
    tokens = parts * rows
    local = local.reshape(3 * tokens, head_width)
    key_value = lax.all_to_all(
        spread_to(local[tokens:], lax.axis_size(KEY_AXES)),
        KEY_AXES, split_axis=0, concat_axis=0, tiled=True,
    )
    group = local[:tokens][None]
    for axis in reversed(QUERY_AXES):
        group = lax.all_gather(group, axis, axis=0, tiled=True)
    key_value, group = lax.optimization_barrier((key_value, group))
    other = lax.ppermute(key_value, "c", [(0, 1), (1, 0)])
    partial = pl.pallas_call(
        attend_kernel,
        out_shape=jax.ShapeDtypeStruct((*group.shape[:2], head_width + HEAD_DIM), jnp.bfloat16),
        in_specs=[pl.BlockSpec(memory_space=pltpu.VMEM)] * 3,
        out_specs=pl.BlockSpec(memory_space=pltpu.VMEM),
        compiler_params=pltpu.CompilerParams(vmem_limit_bytes=KERNEL_VMEM),
        name="attend",
    )(group, key_value, other)
    partial = lax.all_to_all(partial, QUERY_AXES, split_axis=0, concat_axis=0, tiled=True)
    attended = pl.pallas_call(
        combine_kernel,
        out_shape=jax.ShapeDtypeStruct((tokens, head_width), jnp.bfloat16),
        in_specs=[pl.BlockSpec(memory_space=pltpu.VMEM)],
        out_specs=pl.BlockSpec(memory_space=pltpu.VMEM),
        compiler_params=pltpu.CompilerParams(vmem_limit_bytes=KERNEL_VMEM),
        name="combine",
    )(partial)
    parts_attended = lax.all_gather(attended, "tp", axis=0, tiled=False)
    return pl.pallas_call(
        mix_kernel,
        out_shape=jax.ShapeDtypeStruct((tokens, out_weight.shape[1]), jnp.bfloat16),
        in_specs=[
            pl.BlockSpec(memory_space=pltpu.VMEM),
            pl.BlockSpec(memory_space=pltpu.VMEM),
            pl.BlockSpec(memory_space=pltpu.HBM),
        ],
        out_specs=pl.BlockSpec(memory_space=pltpu.VMEM),
        scratch_shapes=[
            pltpu.VMEM(out_weight.shape, out_weight.dtype),
            pltpu.SemaphoreType.DMA((parts * PART_PIECES,)),
        ],
        compiler_params=pltpu.CompilerParams(vmem_limit_bytes=MIX_VMEM),
        name="mix",
    )(parts_attended, gate[None, :], out_weight)


def solution(mesh):
    ctx = ("zl", "y", "x", "c")
    fine = Mesh(mesh.devices.reshape(3, 8, 4, 2, 4), (*ctx, "tp"))
    return jax.shard_map(
        on_device,
        mesh=fine,
        in_specs=(
            P((*ctx, "tp"), None),
            P((*ctx, "tp"), None),
            P((*ctx, "tp"), None),
            P(None, "tp"),
            P("tp"),
        ),
        out_specs=P(ctx, "tp"),
        check_vma=False,
    )
```

```python
import jax
import jax.numpy as jnp
from jax import lax
from jax.experimental import pallas as pl
from jax.experimental.pallas import tpu as pltpu
from jax.sharding import Mesh, PartitionSpec as P

HEAD_DIM = 128
LOG2E = 1.4426950408889634
SCALE = HEAD_DIM ** -0.5
QUERY_AXES = ("zl", "x")
KEY_AXES = ("y",)
SUM_LANE = 8
PIECE_LANES = 16
PART_PIECES = 2
MIX_VMEM = 50 * 1024 * 1024
KERNEL_VMEM = 16 * 1024 * 1024


def split_pieces(stats):
    high = stats.astype(jnp.bfloat16).astype(jnp.float32)
    rest = stats - high
    middle = rest.astype(jnp.bfloat16).astype(jnp.float32)
    low = rest - middle
    lane = lax.broadcasted_iota(jnp.int32, stats.shape, 1)
    spread = jnp.where(
        lane < PIECE_LANES,
        high,
        jnp.where(
            lane < 2 * PIECE_LANES,
            pltpu.roll(middle, PIECE_LANES, 1),
            pltpu.roll(low, 2 * PIECE_LANES, 1),
        ),
    )
    return spread.astype(jnp.bfloat16)


def attend_kernel(q_ref, own_ref, other_ref, out_ref):
    groups, tokens, width = q_ref.shape
    heads = width // HEAD_DIM
    rows = groups * tokens
    lane = lax.broadcasted_iota(jnp.int32, (rows, HEAD_DIM), 1)
    stats = jnp.zeros((rows, HEAD_DIM), jnp.float32)
    for head in range(heads):
        columns = pl.ds(head * HEAD_DIM, HEAD_DIM)
        query = q_ref[:, :, columns].reshape(rows, HEAD_DIM)
        scores, values = [], []
        for ref in (own_ref, other_ref):
            half = ref.shape[1] // 2
            key = ref[:, :half, columns].reshape(ref.shape[0] * half, HEAD_DIM)
            values.append(ref[:, half:, columns].reshape(ref.shape[0] * half, HEAD_DIM))
            scores.append(
                lax.dot_general(
                    query, key, (((1,), (1,)), ((), ())), preferred_element_type=jnp.float32
                )
            )
        highest = jnp.maximum(
            jnp.max(scores[0], axis=1, keepdims=True), jnp.max(scores[1], axis=1, keepdims=True)
        )
        total = jnp.zeros((rows, 1), jnp.float32)
        summed = jnp.zeros((rows, HEAD_DIM), jnp.float32)
        for score, value in zip(scores, values):
            expd = jnp.exp2((score - highest) * (SCALE * LOG2E))
            total += jnp.sum(expd, axis=1, keepdims=True)
            summed += jnp.dot(
                expd.astype(jnp.bfloat16), value, preferred_element_type=jnp.float32
            )
        out_ref[:, :, columns] = summed.astype(jnp.bfloat16).reshape(groups, tokens, HEAD_DIM)
        stats = jnp.where(lane == head, highest, stats)
        stats = jnp.where(lane == SUM_LANE + head, total, stats)
    out_ref[:, :, pl.ds(width, HEAD_DIM)] = split_pieces(stats).reshape(groups, tokens, HEAD_DIM)


def combine_kernel(part_ref, own_ref, out_ref):
    groups, tokens, width = part_ref.shape
    width = width - HEAD_DIM
    heads = width // HEAD_DIM
    pieces = part_ref[:, :, pl.ds(width, HEAD_DIM)].astype(jnp.float32)
    pieces = pieces.reshape(groups * tokens, HEAD_DIM)
    stats = (
        pieces
        + pltpu.roll(pieces, HEAD_DIM - PIECE_LANES, 1)
        + pltpu.roll(pieces, HEAD_DIM - 2 * PIECE_LANES, 1)
    )
    maxima = stats.reshape(groups, tokens, HEAD_DIM)
    sums = pltpu.roll(stats, HEAD_DIM - SUM_LANE, 1).reshape(groups, tokens, HEAD_DIM)
    highest = jnp.max(maxima, axis=0, keepdims=True)
    weight = jnp.exp2((maxima - highest) * (SCALE * LOG2E))
    total = jnp.sum(weight * sums, axis=0)
    for head in range(heads):
        columns = pl.ds(head * HEAD_DIM, HEAD_DIM)
        part = part_ref[:, :, columns].astype(jnp.float32)
        summed = jnp.sum(part * weight[:, :, head : head + 1], axis=0)
        attended = (summed / total[:, head : head + 1]).astype(jnp.bfloat16)
        own_ref[0, :, columns] = attended
        for copy in range(out_ref.shape[0]):
            out_ref[copy, :, columns] = attended


def start_load(weight_ref, held_ref, semaphores, part, slot):
    width = held_ref.shape[1]
    depth = width // PART_PIECES
    copies = []
    for piece in range(PART_PIECES):
        copy = pltpu.make_async_copy(
            weight_ref.at[pl.ds(part * width + piece * depth, depth)],
            held_ref.at[slot, pl.ds(piece * depth, depth)],
            semaphores.at[slot, piece],
        )
        copy.start()
        copies.append(copy)
    return copies


def mix_part(attended_ref, held_ref, copies, part, slot):
    depth = held_ref.shape[1] // PART_PIECES
    product = jnp.zeros((attended_ref.shape[1], held_ref.shape[2]), jnp.float32)
    for piece, copy in enumerate(copies):
        copy.wait()
        span = pl.ds(piece * depth, depth)
        product += jnp.dot(
            attended_ref[part, :, span],
            held_ref[slot, span],
            preferred_element_type=jnp.float32,
        )
    return product


def mix_own_kernel(attended_ref, weight_ref, out_ref, held_ref, semaphores):
    copies = start_load(weight_ref, held_ref, semaphores, lax.axis_index("tp"), 0)
    out_ref[...] = mix_part(attended_ref, held_ref, copies, 0, 0)


def mix_rest_kernel(attended_ref, own_ref, gate_ref, weight_ref, out_ref, held_ref, semaphores):
    parts = attended_ref.shape[0]
    others = [lax.rem(lax.axis_index("tp") + step, parts) for step in range(1, parts)]
    loads = [
        start_load(weight_ref, held_ref, semaphores, part, slot) for slot, part in enumerate(others)
    ]
    product = own_ref[...]
    for slot, part in enumerate(others):
        product += mix_part(attended_ref, held_ref, loads[slot], part, slot)
    out_ref[...] = (product * gate_ref[...]).astype(jnp.bfloat16)


def spread_to(block, count):
    return jnp.broadcast_to(block[None], (count, *block.shape))


def on_device(queries, keys, vals, out_weight, gate):
    parts = lax.axis_size("tp")
    rows, width = queries.shape
    head_width = width // parts
    stacked = jnp.stack([queries, keys, vals], axis=0)
    stacked = stacked.reshape(3, rows, parts, head_width).transpose(2, 0, 1, 3)
    stacked = stacked.reshape(parts, 3 * rows, head_width)
    local = lax.all_to_all(stacked, "tp", split_axis=0, concat_axis=0, tiled=True)
    local = local.reshape(parts, 3, rows, head_width).transpose(1, 0, 2, 3)
    tokens = parts * rows
    local = local.reshape(3 * tokens, head_width)
    key_value = lax.all_to_all(
        spread_to(local[tokens:], lax.axis_size(KEY_AXES)),
        KEY_AXES, split_axis=0, concat_axis=0, tiled=True,
    )
    group = local[:tokens][None]
    for axis in reversed(QUERY_AXES):
        group = lax.all_gather(group, axis, axis=0, tiled=True)
    key_value, group = lax.optimization_barrier((key_value, group))
    other = lax.ppermute(key_value, "c", [(0, 1), (1, 0)])
    partial = pl.pallas_call(
        attend_kernel,
        out_shape=jax.ShapeDtypeStruct((*group.shape[:2], head_width + HEAD_DIM), jnp.bfloat16),
        in_specs=[pl.BlockSpec(memory_space=pltpu.VMEM)] * 3,
        out_specs=pl.BlockSpec(memory_space=pltpu.VMEM),
        compiler_params=pltpu.CompilerParams(vmem_limit_bytes=KERNEL_VMEM),
        name="attend",
    )(group, key_value, other)
    partial = lax.all_to_all(partial, QUERY_AXES, split_axis=0, concat_axis=0, tiled=True)
    own, attended = pl.pallas_call(
        combine_kernel,
        out_shape=[
            jax.ShapeDtypeStruct((1, tokens, head_width), jnp.bfloat16),
            jax.ShapeDtypeStruct((parts, tokens, head_width), jnp.bfloat16),
        ],
        in_specs=[pl.BlockSpec(memory_space=pltpu.VMEM)],
        out_specs=[pl.BlockSpec(memory_space=pltpu.VMEM)] * 2,
        compiler_params=pltpu.CompilerParams(vmem_limit_bytes=KERNEL_VMEM),
        name="combine",
    )(partial)
    channels = out_weight.shape[1]
    product = pl.pallas_call(
        mix_own_kernel,
        out_shape=jax.ShapeDtypeStruct((tokens, channels), jnp.float32),
        in_specs=[
            pl.BlockSpec(memory_space=pltpu.VMEM),
            pl.BlockSpec(memory_space=pltpu.HBM),
        ],
        out_specs=pl.BlockSpec(memory_space=pltpu.VMEM),
        scratch_shapes=[
            pltpu.VMEM((1, head_width, channels), out_weight.dtype),
            pltpu.SemaphoreType.DMA((1, PART_PIECES)),
        ],
        compiler_params=pltpu.CompilerParams(vmem_limit_bytes=MIX_VMEM),
        cost_estimate=pl.CostEstimate(
            flops=2 * tokens * head_width * channels,
            bytes_accessed=head_width * channels * 2,
            transcendentals=0,
        ),
        name="mix_own",
    )(own, out_weight)
    attended = lax.all_to_all(attended, "tp", split_axis=0, concat_axis=0, tiled=True)
    attended, product = lax.optimization_barrier((attended, product))
    return pl.pallas_call(
        mix_rest_kernel,
        out_shape=jax.ShapeDtypeStruct((tokens, channels), jnp.bfloat16),
        in_specs=[
            pl.BlockSpec(memory_space=pltpu.VMEM),
            pl.BlockSpec(memory_space=pltpu.VMEM),
            pl.BlockSpec(memory_space=pltpu.VMEM),
            pl.BlockSpec(memory_space=pltpu.HBM),
        ],
        out_specs=pl.BlockSpec(memory_space=pltpu.VMEM),
        scratch_shapes=[
            pltpu.VMEM((parts - 1, head_width, channels), out_weight.dtype),
            pltpu.SemaphoreType.DMA((parts - 1, PART_PIECES)),
        ],
        compiler_params=pltpu.CompilerParams(vmem_limit_bytes=MIX_VMEM),
        name="mix_rest",
    )(attended, product, gate[None, :], out_weight)


def solution(mesh):
    ctx = ("zl", "y", "x", "c")
    fine = Mesh(mesh.devices.reshape(3, 8, 4, 2, 4), (*ctx, "tp"))
    return jax.shard_map(
        on_device,
        mesh=fine,
        in_specs=(
            P((*ctx, "tp"), None),
            P((*ctx, "tp"), None),
            P((*ctx, "tp"), None),
            P(None, "tp"),
            P("tp"),
        ),
        out_specs=P(ctx, "tp"),
        check_vma=False,
    )
```

```python
import functools

import jax
import jax.numpy as jnp
from jax import lax
from jax.experimental import pallas as pl
from jax.experimental.pallas import tpu as pltpu
from jax.sharding import Mesh, PartitionSpec as P

HEAD_DIM = 128
LOG2E = 1.4426950408889634
SCALE = HEAD_DIM ** -0.5
QUERY_AXES = ("zl", "x")
KEY_AXES = ("y",)
SUM_LANE = 8
PIECE_LANES = 16
PART_PIECES = 2
MIX_VMEM = 50 * 1024 * 1024
KERNEL_VMEM = 16 * 1024 * 1024


def split_pieces(stats):
    high = stats.astype(jnp.bfloat16).astype(jnp.float32)
    rest = stats - high
    middle = rest.astype(jnp.bfloat16).astype(jnp.float32)
    low = rest - middle
    lane = lax.broadcasted_iota(jnp.int32, stats.shape, 1)
    spread = jnp.where(
        lane < PIECE_LANES,
        high,
        jnp.where(
            lane < 2 * PIECE_LANES,
            pltpu.roll(middle, PIECE_LANES, 1),
            pltpu.roll(low, 2 * PIECE_LANES, 1),
        ),
    )
    return spread.astype(jnp.bfloat16)


def attend_kernel(q_ref, own_ref, other_ref, out_ref):
    groups, tokens, width = q_ref.shape
    heads = width // HEAD_DIM
    rows = groups * tokens
    lane = lax.broadcasted_iota(jnp.int32, (rows, HEAD_DIM), 1)
    stats = jnp.zeros((rows, HEAD_DIM), jnp.float32)
    for head in range(heads):
        columns = pl.ds(head * HEAD_DIM, HEAD_DIM)
        query = q_ref[:, :, columns].reshape(rows, HEAD_DIM)
        scores, values = [], []
        for ref in (own_ref, other_ref):
            half = ref.shape[1] // 2
            key = ref[:, :half, columns].reshape(ref.shape[0] * half, HEAD_DIM)
            values.append(ref[:, half:, columns].reshape(ref.shape[0] * half, HEAD_DIM))
            scores.append(
                lax.dot_general(
                    query, key, (((1,), (1,)), ((), ())), preferred_element_type=jnp.float32
                )
            )
        highest = jnp.maximum(
            jnp.max(scores[0], axis=1, keepdims=True), jnp.max(scores[1], axis=1, keepdims=True)
        )
        total = jnp.zeros((rows, 1), jnp.float32)
        summed = jnp.zeros((rows, HEAD_DIM), jnp.float32)
        for score, value in zip(scores, values):
            expd = jnp.exp2((score - highest) * (SCALE * LOG2E))
            total += jnp.sum(expd, axis=1, keepdims=True)
            summed += jnp.dot(
                expd.astype(jnp.bfloat16), value, preferred_element_type=jnp.float32
            )
        out_ref[:, :, columns] = summed.astype(jnp.bfloat16).reshape(groups, tokens, HEAD_DIM)
        stats = jnp.where(lane == head, highest, stats)
        stats = jnp.where(lane == SUM_LANE + head, total, stats)
    out_ref[:, :, pl.ds(width, HEAD_DIM)] = split_pieces(stats).reshape(groups, tokens, HEAD_DIM)


def combine_kernel(part_ref, out_ref):
    groups, tokens, width = part_ref.shape
    width = width - HEAD_DIM
    heads = width // HEAD_DIM
    pieces = part_ref[:, :, pl.ds(width, HEAD_DIM)].astype(jnp.float32)
    pieces = pieces.reshape(groups * tokens, HEAD_DIM)
    stats = (
        pieces
        + pltpu.roll(pieces, HEAD_DIM - PIECE_LANES, 1)
        + pltpu.roll(pieces, HEAD_DIM - 2 * PIECE_LANES, 1)
    )
    maxima = stats.reshape(groups, tokens, HEAD_DIM)
    sums = pltpu.roll(stats, HEAD_DIM - SUM_LANE, 1).reshape(groups, tokens, HEAD_DIM)
    highest = jnp.max(maxima, axis=0, keepdims=True)
    weight = jnp.exp2((maxima - highest) * (SCALE * LOG2E))
    total = jnp.sum(weight * sums, axis=0)
    for head in range(heads):
        columns = pl.ds(head * HEAD_DIM, HEAD_DIM)
        part = part_ref[:, :, columns].astype(jnp.float32)
        summed = jnp.sum(part * weight[:, :, head : head + 1], axis=0)
        attended = (summed / total[:, head : head + 1]).astype(jnp.bfloat16)
        out_ref[:, columns] = attended


def start_load(weight_ref, held_ref, semaphores, part, slot):
    width = held_ref.shape[1]
    depth = width // PART_PIECES
    copies = []
    for piece in range(PART_PIECES):
        copy = pltpu.make_async_copy(
            weight_ref.at[pl.ds(part * width + piece * depth, depth)],
            held_ref.at[slot, pl.ds(piece * depth, depth)],
            semaphores.at[slot, piece],
        )
        copy.start()
        copies.append(copy)
    return copies


def mix_part(attended_ref, held_ref, copies, slot):
    depth = held_ref.shape[1] // PART_PIECES
    product = jnp.zeros((attended_ref.shape[0], held_ref.shape[2]), jnp.float32)
    for piece, copy in enumerate(copies):
        copy.wait()
        span = pl.ds(piece * depth, depth)
        product += jnp.dot(
            attended_ref[:, span],
            held_ref[slot, span],
            preferred_element_type=jnp.float32,
        )
    return product


def mix_kernel(steps, *refs):
    count = len(steps)
    attended_refs, (weight_ref, *more, out_ref, held_ref, semaphores) = refs[:count], refs[count:]
    parts = weight_ref.shape[0] // held_ref.shape[1]
    loads = [
        start_load(
            weight_ref, held_ref, semaphores, lax.rem(lax.axis_index("tp") + step, parts), slot
        )
        for slot, step in enumerate(steps)
    ]
    product = more[0][...] if more else jnp.zeros(out_ref.shape, jnp.float32)
    for slot, attended_ref in enumerate(attended_refs):
        product += mix_part(attended_ref, held_ref, loads[slot], slot)
    if len(more) > 1:
        product *= more[1][...]
    out_ref[...] = product.astype(out_ref.dtype)


def mix(steps, attended, weight, more, dtype):
    tokens, width = attended[0].shape
    channels = weight.shape[1]
    in_vmem = pl.BlockSpec(memory_space=pltpu.VMEM)
    return pl.pallas_call(
        functools.partial(mix_kernel, steps),
        out_shape=jax.ShapeDtypeStruct((tokens, channels), dtype),
        in_specs=[in_vmem] * len(steps)
        + [pl.BlockSpec(memory_space=pltpu.HBM)]
        + [in_vmem] * len(more),
        out_specs=in_vmem,
        scratch_shapes=[
            pltpu.VMEM((len(steps), width, channels), weight.dtype),
            pltpu.SemaphoreType.DMA((len(steps), PART_PIECES)),
        ],
        compiler_params=pltpu.CompilerParams(vmem_limit_bytes=MIX_VMEM),
        cost_estimate=pl.CostEstimate(
            flops=2 * len(steps) * tokens * width * channels,
            bytes_accessed=2 * len(steps) * width * channels,
            transcendentals=0,
        ),
        name="mix",
    )(*attended, weight, *more)


def spread_to(block, count):
    return jnp.broadcast_to(block[None], (count, *block.shape))


def on_device(queries, keys, vals, out_weight, gate):
    parts = lax.axis_size("tp")
    rows, width = queries.shape
    head_width = width // parts
    stacked = jnp.stack([queries, keys, vals], axis=0)
    stacked = stacked.reshape(3, rows, parts, head_width).transpose(2, 0, 1, 3)
    stacked = stacked.reshape(parts, 3 * rows, head_width)
    local = lax.all_to_all(stacked, "tp", split_axis=0, concat_axis=0, tiled=True)
    local = local.reshape(parts, 3, rows, head_width).transpose(1, 0, 2, 3)
    tokens = parts * rows
    local = local.reshape(3 * tokens, head_width)
    key_value = lax.all_to_all(
        spread_to(local[tokens:], lax.axis_size(KEY_AXES)),
        KEY_AXES, split_axis=0, concat_axis=0, tiled=True,
    )
    group = lax.all_gather(local[:tokens], QUERY_AXES, axis=0, tiled=False)
    key_value, group = lax.optimization_barrier((key_value, group))
    other = lax.ppermute(key_value, "c", [(0, 1), (1, 0)])
    partial = pl.pallas_call(
        attend_kernel,
        out_shape=jax.ShapeDtypeStruct((*group.shape[:2], head_width + HEAD_DIM), jnp.bfloat16),
        in_specs=[pl.BlockSpec(memory_space=pltpu.VMEM)] * 3,
        out_specs=pl.BlockSpec(memory_space=pltpu.VMEM),
        compiler_params=pltpu.CompilerParams(vmem_limit_bytes=KERNEL_VMEM),
        name="attend",
    )(group, key_value, other)
    partial = lax.all_to_all(partial, QUERY_AXES, split_axis=0, concat_axis=0, tiled=True)
    attended = pl.pallas_call(
        combine_kernel,
        out_shape=jax.ShapeDtypeStruct((tokens, head_width), jnp.bfloat16),
        in_specs=[pl.BlockSpec(memory_space=pltpu.VMEM)],
        out_specs=pl.BlockSpec(memory_space=pltpu.VMEM),
        compiler_params=pltpu.CompilerParams(vmem_limit_bytes=KERNEL_VMEM),
        name="combine",
    )(partial)

    def from_ahead(step):
        pairs = [(place, (place - step) % parts) for place in range(parts)]
        return lax.ppermute(attended, "tp", pairs)

    arrived = {step: from_ahead(step) for step in (2, 1, 3)}
    product = mix((0,), [attended], out_weight, [], jnp.float32)
    product = mix((1, 3), [arrived[1], arrived[3]], out_weight, [product], jnp.float32)
    return mix((2,), [arrived[2]], out_weight, [product, gate[None, :]], jnp.bfloat16)


def solution(mesh):
    ctx = ("zl", "y", "x", "c")
    fine = Mesh(mesh.devices.reshape(3, 8, 4, 2, 4), (*ctx, "tp"))
    return jax.shard_map(
        on_device,
        mesh=fine,
        in_specs=(
            P((*ctx, "tp"), None),
            P((*ctx, "tp"), None),
            P((*ctx, "tp"), None),
            P(None, "tp"),
            P("tp"),
        ),
        out_specs=P(ctx, "tp"),
        check_vma=False,
    )
```

```python
import jax
import jax.numpy as jnp
from jax import lax
from jax.experimental import pallas as pl
from jax.experimental.pallas import tpu as pltpu
from jax.sharding import Mesh, PartitionSpec as P

HEAD_DIM = 128
LOG2E = 1.4426950408889634
SCALE = HEAD_DIM ** -0.5
HEAD_AXES = ("zl", "c", "tp")
QUERY_AXES = ("x",)
KEY_AXES = ("y",)
PIECE_LANES = 8
KERNEL_VMEM = 16 * 1024 * 1024
MIX_VMEM = 50 * 1024 * 1024
IN_VMEM = pl.BlockSpec(memory_space=pltpu.VMEM)


def split_pieces(stats):
    high = stats.astype(jnp.bfloat16).astype(jnp.float32)
    rest = stats - high
    middle = rest.astype(jnp.bfloat16).astype(jnp.float32)
    low = rest - middle
    lane = lax.broadcasted_iota(jnp.int32, stats.shape, 1)
    spread = jnp.where(
        lane < PIECE_LANES,
        high,
        jnp.where(
            lane < 2 * PIECE_LANES,
            pltpu.roll(middle, PIECE_LANES, 1),
            pltpu.roll(low, 2 * PIECE_LANES, 1),
        ),
    )
    return spread.astype(jnp.bfloat16)


def attend_kernel(q_ref, key_value_ref, out_ref):
    groups, tokens, width = q_ref.shape
    count = key_value_ref.shape[0] * tokens
    key = key_value_ref[:, 0].reshape(count, width)
    value = key_value_ref[:, 1].reshape(count, width)
    lane = lax.broadcasted_iota(jnp.int32, (tokens, HEAD_DIM), 1)
    for group in range(groups):
        score = lax.dot_general(
            q_ref[group], key, (((1,), (1,)), ((), ())), preferred_element_type=jnp.float32
        )
        highest = jnp.max(score, axis=1, keepdims=True)
        expd = jnp.exp2((score - highest) * (SCALE * LOG2E))
        total = jnp.sum(expd, axis=1, keepdims=True)
        summed = jnp.dot(expd.astype(jnp.bfloat16), value, preferred_element_type=jnp.float32)
        out_ref[group, :, pl.ds(0, width)] = summed.astype(jnp.bfloat16)
        stats = jnp.where(lane == 0, highest, jnp.where(lane == 1, total, 0.0))
        out_ref[group, :, pl.ds(width, HEAD_DIM)] = split_pieces(stats)


def combine_kernel(part_ref, out_ref):
    groups, tokens, _ = part_ref.shape
    copies, rows, width = out_ref.shape
    pieces = part_ref[:, :, pl.ds(width, HEAD_DIM)].astype(jnp.float32)
    pieces = pieces.reshape(groups * tokens, HEAD_DIM)
    stats = (
        pieces
        + pltpu.roll(pieces, HEAD_DIM - PIECE_LANES, 1)
        + pltpu.roll(pieces, HEAD_DIM - 2 * PIECE_LANES, 1)
    ).reshape(groups, tokens, HEAD_DIM)
    maxima, sums = stats[:, :, 0:1], stats[:, :, 1:2]
    weight = jnp.exp2((maxima - jnp.max(maxima, axis=0, keepdims=True)) * (SCALE * LOG2E))
    total = jnp.sum(weight * sums, axis=0)
    summed = jnp.sum(part_ref[:, :, pl.ds(0, width)].astype(jnp.float32) * weight, axis=0)
    attended = (summed / total).astype(jnp.bfloat16)
    repeats = copies * rows // tokens
    for block in range(tokens // rows):
        for repeat in range(repeats):
            out_ref[block * repeats + repeat] = attended[block * rows : (block + 1) * rows]


def mix_kernel(attended_ref, gate_ref, weight_ref, out_ref, held_ref, semaphores):
    heads = weight_ref.shape[0] // HEAD_DIM
    pieces = semaphores.shape[0]
    span = heads // pieces
    copies = []
    for piece in range(pieces):
        rows = pl.ds(piece * span * HEAD_DIM, span * HEAD_DIM)
        copy = pltpu.make_async_copy(weight_ref.at[rows], held_ref.at[rows], semaphores.at[piece])
        copy.start()
        copies.append(copy)
    product = jnp.zeros(out_ref.shape, jnp.float32)
    for piece, copy in enumerate(copies):
        first = piece * span
        block = jnp.concatenate(
            [attended_ref[head] for head in range(first, first + span)], axis=1
        )
        copy.wait()
        product += jnp.dot(
            block,
            held_ref[pl.ds(first * HEAD_DIM, span * HEAD_DIM)],
            preferred_element_type=jnp.float32,
        )
    out_ref[...] = (product * gate_ref[...]).astype(jnp.bfloat16)


def exchange(blocks, axes):
    return lax.all_to_all(blocks, axes, split_axis=0, concat_axis=0, tiled=True)


def spread_to(block, count):
    return jnp.broadcast_to(block[None], (count, *block.shape))


def on_device(queries, keys, vals, out_weight, gate):
    slots = lax.axis_size(HEAD_AXES)
    rows, width = queries.shape
    heads = width // HEAD_DIM
    tokens = slots * rows
    own_tokens = lax.axis_size("tp") * rows
    stacked = jnp.stack([queries, keys, vals], axis=0).reshape(3, rows, heads, HEAD_DIM)
    stacked = stacked.transpose(2, 0, 1, 3).reshape(heads, 3 * rows, HEAD_DIM)
    stacked = jnp.pad(stacked, ((0, slots - heads), (0, 0), (0, 0)))
    local = exchange(stacked, HEAD_AXES)
    local = local.reshape(slots, 3, rows, HEAD_DIM).transpose(1, 0, 2, 3)
    local = local.reshape(3, tokens, HEAD_DIM)
    key_value = exchange(spread_to(local[1:], lax.axis_size(KEY_AXES)), KEY_AXES)
    group = lax.all_gather(local[0], QUERY_AXES, axis=0, tiled=False)
    key_value, group = lax.optimization_barrier((key_value, group))
    partial = pl.pallas_call(
        attend_kernel,
        out_shape=jax.ShapeDtypeStruct((*group.shape[:2], 2 * HEAD_DIM), jnp.bfloat16),
        in_specs=[IN_VMEM] * 2,
        out_specs=IN_VMEM,
        compiler_params=pltpu.CompilerParams(vmem_limit_bytes=KERNEL_VMEM),
        name="attend",
    )(group, key_value)
    partial = exchange(partial, QUERY_AXES)
    attended = pl.pallas_call(
        combine_kernel,
        out_shape=jax.ShapeDtypeStruct((slots, own_tokens, HEAD_DIM), jnp.bfloat16),
        in_specs=[IN_VMEM],
        out_specs=IN_VMEM,
        compiler_params=pltpu.CompilerParams(vmem_limit_bytes=KERNEL_VMEM),
        name="combine",
    )(partial)
    attended = exchange(attended, HEAD_AXES)
    return pl.pallas_call(
        mix_kernel,
        out_shape=jax.ShapeDtypeStruct((own_tokens, out_weight.shape[1]), jnp.bfloat16),
        in_specs=[IN_VMEM, IN_VMEM, pl.BlockSpec(memory_space=pltpu.HBM)],
        out_specs=IN_VMEM,
        scratch_shapes=[
            pltpu.VMEM(out_weight.shape, out_weight.dtype),
            pltpu.SemaphoreType.DMA((heads // 2,)),
        ],
        compiler_params=pltpu.CompilerParams(vmem_limit_bytes=MIX_VMEM),
        name="mix",
    )(attended, gate[None, :], out_weight)


def solution(mesh):
    ctx = ("zl", "y", "x", "c")
    fine = Mesh(mesh.devices.reshape(3, 8, 4, 2, 4), (*ctx, "tp"))
    return jax.shard_map(
        on_device,
        mesh=fine,
        in_specs=(
            P((*ctx, "tp"), None),
            P((*ctx, "tp"), None),
            P((*ctx, "tp"), None),
            P(None, "tp"),
            P("tp"),
        ),
        out_specs=P(ctx, "tp"),
        check_vma=False,
    )
```

```python
import jax
import jax.numpy as jnp
from jax import lax
from jax.experimental import pallas as pl
from jax.experimental.pallas import tpu as pltpu
from jax.sharding import Mesh, PartitionSpec as P

HEAD_DIM = 128
LOG2E = 1.4426950408889634
SCALE = HEAD_DIM ** -0.5
HEAD_AXES = ("zl", "c", "tp")
QUERY_AXES = ("y",)
KEY_AXES = ("x",)
STATS = 2
STAT_LANES = 8
STAT_ROWS = 16
KERNEL_VMEM = 16 * 1024 * 1024
MIX_VMEM = 50 * 1024 * 1024
IN_VMEM = pl.BlockSpec(memory_space=pltpu.VMEM)


def pack_stats(highest, total):
    tokens = highest.shape[0]
    lane = lax.broadcasted_iota(jnp.int32, (tokens, HEAD_DIM), 1)
    stats = jnp.where(lane == 0, highest, jnp.where(lane == 1, total, 0.0))
    high = stats.astype(jnp.bfloat16).astype(jnp.float32)
    rest = stats - high
    middle = rest.astype(jnp.bfloat16).astype(jnp.float32)
    low = rest - middle
    pieces = high + pltpu.roll(middle, STATS, 1) + pltpu.roll(low, 2 * STATS, 1)
    filler = jnp.zeros((2 * HEAD_DIM - tokens, HEAD_DIM), jnp.float32)
    rows = jnp.concatenate([pieces, filler], axis=0).T[:STAT_LANES]
    return jnp.concatenate([rows[:, :HEAD_DIM], rows[:, HEAD_DIM:]], axis=0).astype(jnp.bfloat16)


def unpack_stats(packed, tokens):
    groups = packed.shape[0]
    rows = packed.astype(jnp.float32)
    filler = jnp.zeros((HEAD_DIM - groups * STAT_LANES, HEAD_DIM), jnp.float32)
    halves = [
        jnp.concatenate(
            [rows[group, half : half + STAT_LANES] for group in range(groups)] + [filler], axis=0
        )
        for half in (0, STAT_LANES)
    ]
    pieces = jnp.concatenate([half.T for half in halves], axis=0)[:tokens]
    return (
        pieces
        + pltpu.roll(pieces, HEAD_DIM - STATS, 1)
        + pltpu.roll(pieces, HEAD_DIM - 2 * STATS, 1)
    )


def attend_kernel(q_ref, key_value_ref, out_ref):
    groups, tokens, width = q_ref.shape
    count = key_value_ref.shape[0] * tokens
    key = key_value_ref[:, 0].reshape(count, width)
    value = key_value_ref[:, 1].reshape(count, width)
    for group in range(groups):
        score = lax.dot_general(
            q_ref[group], key, (((1,), (1,)), ((), ())), preferred_element_type=jnp.float32
        )
        highest = jnp.max(score, axis=1, keepdims=True)
        expd = jnp.exp2((score - highest) * (SCALE * LOG2E))
        total = jnp.sum(expd, axis=1, keepdims=True)
        summed = jnp.dot(expd.astype(jnp.bfloat16), value, preferred_element_type=jnp.float32)
        out_ref[group, pl.ds(0, tokens)] = summed.astype(jnp.bfloat16)
        out_ref[group, pl.ds(tokens, STAT_ROWS)] = pack_stats(highest, total)


def combine_kernel(part_ref, out_ref):
    groups = part_ref.shape[0]
    tokens = part_ref.shape[1] - STAT_ROWS
    copies, rows, _ = out_ref.shape
    stats = unpack_stats(part_ref[:, pl.ds(tokens, STAT_ROWS)], tokens)
    lane = lax.broadcasted_iota(jnp.int32, stats.shape, 1)
    is_maximum = (lane % STAT_LANES == 0) & (lane < groups * STAT_LANES)
    highest = jnp.max(jnp.where(is_maximum, stats, -jnp.inf), axis=1, keepdims=True)
    weight = jnp.where(is_maximum, jnp.exp2((stats - highest) * (SCALE * LOG2E)), 0.0)
    sums = jnp.where(is_maximum, pltpu.roll(stats, HEAD_DIM - 1, 1), 0.0)
    total = jnp.sum(weight * sums, axis=1, keepdims=True)
    summed = jnp.zeros(stats.shape, jnp.float32)
    for group in range(groups):
        at = group * STAT_LANES
        part = part_ref[group, pl.ds(0, tokens)].astype(jnp.float32)
        summed += part * weight[:, at : at + 1]
    attended = (summed / total).astype(jnp.bfloat16)
    repeats = copies * rows // tokens
    for block in range(tokens // rows):
        for repeat in range(repeats):
            out_ref[block * repeats + repeat] = attended[block * rows : (block + 1) * rows]


def mix_kernel(attended_ref, gate_ref, weight_ref, out_ref, held_ref, semaphores):
    heads = weight_ref.shape[0] // HEAD_DIM
    pieces = semaphores.shape[0]
    span = heads // pieces
    copies = []
    for piece in range(pieces):
        rows = pl.ds(piece * span * HEAD_DIM, span * HEAD_DIM)
        copy = pltpu.make_async_copy(weight_ref.at[rows], held_ref.at[rows], semaphores.at[piece])
        copy.start()
        copies.append(copy)
    product = jnp.zeros(out_ref.shape, jnp.float32)
    for piece, copy in enumerate(copies):
        first = piece * span
        block = jnp.concatenate(
            [attended_ref[head] for head in range(first, first + span)], axis=1
        )
        copy.wait()
        product += jnp.dot(
            block,
            held_ref[pl.ds(first * HEAD_DIM, span * HEAD_DIM)],
            preferred_element_type=jnp.float32,
        )
    out_ref[...] = (product * gate_ref[...]).astype(jnp.bfloat16)


def exchange(blocks, axes):
    return lax.all_to_all(blocks, axes, split_axis=0, concat_axis=0, tiled=True)


def spread_to(block, count):
    return jnp.broadcast_to(block[None], (count, *block.shape))


def on_device(queries, keys, vals, out_weight, gate):
    slots = lax.axis_size(HEAD_AXES)
    rows, width = queries.shape
    heads = width // HEAD_DIM
    tokens = slots * rows
    own_tokens = lax.axis_size("tp") * rows
    stacked = jnp.stack([queries, keys, vals], axis=0).reshape(3, rows, heads, HEAD_DIM)
    stacked = stacked.transpose(2, 0, 1, 3).reshape(heads, 3 * rows, HEAD_DIM)
    stacked = jnp.pad(stacked, ((0, slots - heads), (0, 0), (0, 0)))
    local = exchange(stacked, HEAD_AXES)
    local = local.reshape(slots, 3, rows, HEAD_DIM).transpose(1, 0, 2, 3)
    local = local.reshape(3, tokens, HEAD_DIM)
    group = exchange(spread_to(local[0], lax.axis_size(QUERY_AXES)), QUERY_AXES)
    key_value = lax.all_gather(local[1:], KEY_AXES, axis=0, tiled=False)
    gate_row = gate[None, :]
    key_value, group, gate_row = lax.optimization_barrier((key_value, group, gate_row))
    partial = pl.pallas_call(
        attend_kernel,
        out_shape=jax.ShapeDtypeStruct(
            (group.shape[0], tokens + STAT_ROWS, HEAD_DIM), jnp.bfloat16
        ),
        in_specs=[IN_VMEM] * 2,
        out_specs=IN_VMEM,
        compiler_params=pltpu.CompilerParams(vmem_limit_bytes=KERNEL_VMEM),
        name="attend",
    )(group, key_value)
    partial = exchange(partial, QUERY_AXES)
    attended = pl.pallas_call(
        combine_kernel,
        out_shape=jax.ShapeDtypeStruct((slots, own_tokens, HEAD_DIM), jnp.bfloat16),
        in_specs=[IN_VMEM],
        out_specs=IN_VMEM,
        compiler_params=pltpu.CompilerParams(vmem_limit_bytes=KERNEL_VMEM),
        name="combine",
    )(partial)
    attended = exchange(attended, HEAD_AXES)
    return pl.pallas_call(
        mix_kernel,
        out_shape=jax.ShapeDtypeStruct((own_tokens, out_weight.shape[1]), jnp.bfloat16),
        in_specs=[IN_VMEM, IN_VMEM, pl.BlockSpec(memory_space=pltpu.HBM)],
        out_specs=IN_VMEM,
        scratch_shapes=[
            pltpu.VMEM(out_weight.shape, out_weight.dtype),
            pltpu.SemaphoreType.DMA((heads // 2,)),
        ],
        compiler_params=pltpu.CompilerParams(vmem_limit_bytes=MIX_VMEM),
        name="mix",
    )(attended, gate_row, out_weight)


def solution(mesh):
    ctx = ("zl", "y", "x", "c")
    fine = Mesh(mesh.devices.reshape(3, 8, 4, 2, 4), (*ctx, "tp"))
    return jax.shard_map(
        on_device,
        mesh=fine,
        in_specs=(
            P((*ctx, "tp"), None),
            P((*ctx, "tp"), None),
            P((*ctx, "tp"), None),
            P(None, "tp"),
            P("tp"),
        ),
        out_specs=P(ctx, "tp"),
        check_vma=False,
    )
```

```python
import jax
import jax.numpy as jnp
from jax import lax
from jax.experimental import pallas as pl
from jax.experimental.pallas import tpu as pltpu
from jax.sharding import Mesh, PartitionSpec as P

HEAD_DIM = 128
LOG2E = 1.4426950408889634
SCALE = HEAD_DIM ** -0.5
HEAD_AXES = ("zl", "c", "tp")
QUERY_AXES = ("y",)
KEY_AXES = ("x",)
STATS = 2
STAT_LANES = 8
STAT_ROWS = 16
GROUP_STEP = 2
KERNEL_VMEM = 16 * 1024 * 1024
MIX_VMEM = 50 * 1024 * 1024
IN_VMEM = pl.BlockSpec(memory_space=pltpu.VMEM)


def pack_stats(columns):
    tokens = columns[0][0].shape[0]
    lane = lax.broadcasted_iota(jnp.int32, (tokens, HEAD_DIM), 1)
    stats = jnp.zeros((tokens, HEAD_DIM), jnp.float32)
    for group, values in enumerate(columns):
        for place, value in enumerate(values):
            stats = jnp.where(lane == group * STAT_LANES + place, value, stats)
    high = stats.astype(jnp.bfloat16).astype(jnp.float32)
    rest = stats - high
    middle = rest.astype(jnp.bfloat16).astype(jnp.float32)
    low = rest - middle
    pieces = high + pltpu.roll(middle, STATS, 1) + pltpu.roll(low, 2 * STATS, 1)
    filler = jnp.zeros((2 * HEAD_DIM - tokens, HEAD_DIM), jnp.float32)
    rows = jnp.concatenate([pieces, filler], axis=0).T
    packed = []
    for group in range(len(columns)):
        own = rows[group * STAT_LANES : (group + 1) * STAT_LANES]
        both = jnp.concatenate([own[:, :HEAD_DIM], own[:, HEAD_DIM:]], axis=0)
        packed.append(both.astype(jnp.bfloat16))
    return packed


def unpack_stats(packed, tokens):
    groups = packed.shape[0]
    rows = packed.astype(jnp.float32)
    filler = jnp.zeros((HEAD_DIM - groups * STAT_LANES, HEAD_DIM), jnp.float32)
    halves = [
        jnp.concatenate(
            [rows[group, half : half + STAT_LANES] for group in range(groups)] + [filler], axis=0
        )
        for half in (0, STAT_LANES)
    ]
    pieces = jnp.concatenate([half.T for half in halves], axis=0)[:tokens]
    return (
        pieces
        + pltpu.roll(pieces, HEAD_DIM - STATS, 1)
        + pltpu.roll(pieces, HEAD_DIM - 2 * STATS, 1)
    )


def split_kernel(local_ref, query_ref, key_value_ref):
    slots = local_ref.shape[0]
    rows = local_ref.shape[1] // 3
    query = local_ref[:, pl.ds(0, rows)].reshape(slots * rows, HEAD_DIM)
    for copy in range(query_ref.shape[0]):
        query_ref[copy] = query
    for place in range(2):
        block = local_ref[:, pl.ds((place + 1) * rows, rows)]
        key_value_ref[place] = block.reshape(slots * rows, HEAD_DIM)


def attend_kernel(q_ref, key_value_ref, out_ref):
    groups, tokens, width = q_ref.shape
    count = key_value_ref.shape[0] * tokens
    key = key_value_ref[:, 0].reshape(count, width)
    value = key_value_ref[:, 1].reshape(count, width)
    columns = []
    for group in range(0, groups, GROUP_STEP):
        query = q_ref[pl.ds(group, GROUP_STEP)].reshape(GROUP_STEP * tokens, width)
        score = lax.dot_general(
            query, key, (((1,), (1,)), ((), ())), preferred_element_type=jnp.float32
        )
        highest = jnp.max(score, axis=1, keepdims=True)
        expd = jnp.exp2((score - highest) * (SCALE * LOG2E))
        total = jnp.sum(expd, axis=1, keepdims=True)
        summed = jnp.dot(expd.astype(jnp.bfloat16), value, preferred_element_type=jnp.float32)
        for step in range(GROUP_STEP):
            rows = slice(step * tokens, (step + 1) * tokens)
            out_ref[group + step, pl.ds(0, tokens)] = summed[rows].astype(jnp.bfloat16)
            columns.append((highest[rows], total[rows]))
    for group, packed in enumerate(pack_stats(columns)):
        out_ref[group, pl.ds(tokens, STAT_ROWS)] = packed


def combine_kernel(part_ref, out_ref):
    groups = part_ref.shape[0]
    tokens = part_ref.shape[1] - STAT_ROWS
    copies, rows, _ = out_ref.shape
    stats = unpack_stats(part_ref[:, pl.ds(tokens, STAT_ROWS)], tokens)
    lane = lax.broadcasted_iota(jnp.int32, stats.shape, 1)
    is_maximum = (lane % STAT_LANES == 0) & (lane < groups * STAT_LANES)
    highest = jnp.max(jnp.where(is_maximum, stats, -jnp.inf), axis=1, keepdims=True)
    weight = jnp.where(is_maximum, jnp.exp2((stats - highest) * (SCALE * LOG2E)), 0.0)
    sums = jnp.where(is_maximum, pltpu.roll(stats, HEAD_DIM - 1, 1), 0.0)
    total = jnp.sum(weight * sums, axis=1, keepdims=True)
    summed = jnp.zeros(stats.shape, jnp.float32)
    for group in range(groups):
        at = group * STAT_LANES
        part = part_ref[group, pl.ds(0, tokens)].astype(jnp.float32)
        summed += part * weight[:, at : at + 1]
    attended = (summed / total).astype(jnp.bfloat16)
    repeats = copies * rows // tokens
    for block in range(tokens // rows):
        for repeat in range(repeats):
            out_ref[block * repeats + repeat] = attended[block * rows : (block + 1) * rows]


def mix_kernel(attended_ref, gate_ref, weight_ref, out_ref, held_ref, semaphores):
    heads = weight_ref.shape[0] // HEAD_DIM
    pieces = semaphores.shape[0]
    span = heads // pieces
    copies = []
    for piece in range(pieces):
        rows = pl.ds(piece * span * HEAD_DIM, span * HEAD_DIM)
        copy = pltpu.make_async_copy(weight_ref.at[rows], held_ref.at[rows], semaphores.at[piece])
        copy.start()
        copies.append(copy)
    product = jnp.zeros(out_ref.shape, jnp.float32)
    for piece, copy in enumerate(copies):
        first = piece * span
        block = jnp.concatenate(
            [attended_ref[head] for head in range(first, first + span)], axis=1
        )
        copy.wait()
        product += jnp.dot(
            block,
            held_ref[pl.ds(first * HEAD_DIM, span * HEAD_DIM)],
            preferred_element_type=jnp.float32,
        )
    out_ref[...] = (product * gate_ref[...][None, :]).astype(jnp.bfloat16)


def exchange(blocks, axes):
    return lax.all_to_all(blocks, axes, split_axis=0, concat_axis=0, tiled=True)


def on_device(queries, keys, vals, out_weight, gate):
    slots = lax.axis_size(HEAD_AXES)
    rows, width = queries.shape
    heads = width // HEAD_DIM
    tokens = slots * rows
    own_tokens = lax.axis_size("tp") * rows
    stacked = jnp.stack([queries, keys, vals], axis=0).reshape(3, rows, heads, HEAD_DIM)
    stacked = stacked.transpose(2, 0, 1, 3).reshape(heads, 3 * rows, HEAD_DIM)
    stacked = jnp.pad(stacked, ((0, slots - heads), (0, 0), (0, 0)))
    query_copies, own_key_value = pl.pallas_call(
        split_kernel,
        out_shape=[
            jax.ShapeDtypeStruct((lax.axis_size(QUERY_AXES), tokens, HEAD_DIM), jnp.bfloat16),
            jax.ShapeDtypeStruct((2, tokens, HEAD_DIM), jnp.bfloat16),
        ],
        in_specs=[IN_VMEM],
        out_specs=[IN_VMEM] * 2,
        compiler_params=pltpu.CompilerParams(vmem_limit_bytes=KERNEL_VMEM),
        name="split",
    )(exchange(stacked, HEAD_AXES))
    group = exchange(query_copies, QUERY_AXES)
    key_value = lax.all_gather(own_key_value, KEY_AXES, axis=0, tiled=False)
    key_value, group = lax.optimization_barrier((key_value, group))
    partial = pl.pallas_call(
        attend_kernel,
        out_shape=jax.ShapeDtypeStruct(
            (group.shape[0], tokens + STAT_ROWS, HEAD_DIM), jnp.bfloat16
        ),
        in_specs=[IN_VMEM] * 2,
        out_specs=IN_VMEM,
        compiler_params=pltpu.CompilerParams(vmem_limit_bytes=KERNEL_VMEM),
        name="attend",
    )(group, key_value)
    partial = exchange(partial, QUERY_AXES)
    attended = pl.pallas_call(
        combine_kernel,
        out_shape=jax.ShapeDtypeStruct((slots, own_tokens, HEAD_DIM), jnp.bfloat16),
        in_specs=[IN_VMEM],
        out_specs=IN_VMEM,
        compiler_params=pltpu.CompilerParams(vmem_limit_bytes=KERNEL_VMEM),
        name="combine",
    )(partial)
    attended = exchange(attended, HEAD_AXES)
    return pl.pallas_call(
        mix_kernel,
        out_shape=jax.ShapeDtypeStruct((own_tokens, out_weight.shape[1]), jnp.bfloat16),
        in_specs=[IN_VMEM, IN_VMEM, pl.BlockSpec(memory_space=pltpu.HBM)],
        out_specs=IN_VMEM,
        scratch_shapes=[
            pltpu.VMEM(out_weight.shape, out_weight.dtype),
            pltpu.SemaphoreType.DMA((heads // 2,)),
        ],
        compiler_params=pltpu.CompilerParams(vmem_limit_bytes=MIX_VMEM),
        name="mix",
    )(attended, gate, out_weight)


def solution(mesh):
    ctx = ("zl", "y", "x", "c")
    fine = Mesh(mesh.devices.reshape(3, 8, 4, 2, 4), (*ctx, "tp"))
    return jax.shard_map(
        on_device,
        mesh=fine,
        in_specs=(
            P((*ctx, "tp"), None),
            P((*ctx, "tp"), None),
            P((*ctx, "tp"), None),
            P(None, "tp"),
            P("tp"),
        ),
        out_specs=P(ctx, "tp"),
        check_vma=False,
    )
```

```python
import jax
import jax.numpy as jnp
from jax import lax
from jax.experimental import pallas as pl
from jax.experimental.pallas import tpu as pltpu
from jax.sharding import Mesh, PartitionSpec as P

HEAD_DIM = 128
LOG2E = 1.4426950408889634
SCALE = HEAD_DIM ** -0.5
HEAD_AXES = ("zl", "c", "tp")
QUERY_AXES = ("y",)
KEY_AXIS = "x"
KEY_PAIRS = ([[0, 1], [2, 3]], [[1, 2], [3, 0]])
STATS = 2
STAT_LANES = 8
STAT_ROWS = 16
GROUP_STEP = 2
KERNEL_VMEM = 16 * 1024 * 1024
MIX_VMEM = 50 * 1024 * 1024
IN_VMEM = pl.BlockSpec(memory_space=pltpu.VMEM)


def pack_stats(columns):
    tokens = columns[0][0].shape[0]
    lane = lax.broadcasted_iota(jnp.int32, (tokens, HEAD_DIM), 1)
    stats = jnp.zeros((tokens, HEAD_DIM), jnp.float32)
    for group, values in enumerate(columns):
        for place, value in enumerate(values):
            stats = jnp.where(lane == group * STAT_LANES + place, value, stats)
    high = stats.astype(jnp.bfloat16).astype(jnp.float32)
    rest = stats - high
    middle = rest.astype(jnp.bfloat16).astype(jnp.float32)
    low = rest - middle
    pieces = high + pltpu.roll(middle, STATS, 1) + pltpu.roll(low, 2 * STATS, 1)
    filler = jnp.zeros((2 * HEAD_DIM - tokens, HEAD_DIM), jnp.float32)
    rows = jnp.concatenate([pieces, filler], axis=0).T
    packed = []
    for group in range(len(columns)):
        own = rows[group * STAT_LANES : (group + 1) * STAT_LANES]
        both = jnp.concatenate([own[:, :HEAD_DIM], own[:, HEAD_DIM:]], axis=0)
        packed.append(both.astype(jnp.bfloat16))
    return packed


def unpack_stats(packed, tokens):
    groups = packed.shape[0]
    rows = packed.astype(jnp.float32)
    filler = jnp.zeros((HEAD_DIM - groups * STAT_LANES, HEAD_DIM), jnp.float32)
    halves = [
        jnp.concatenate(
            [rows[group, half : half + STAT_LANES] for group in range(groups)] + [filler], axis=0
        )
        for half in (0, STAT_LANES)
    ]
    pieces = jnp.concatenate([half.T for half in halves], axis=0)[:tokens]
    return (
        pieces
        + pltpu.roll(pieces, HEAD_DIM - STATS, 1)
        + pltpu.roll(pieces, HEAD_DIM - 2 * STATS, 1)
    )


def split_kernel(local_ref, query_ref, key_value_ref):
    slots = local_ref.shape[0]
    rows = local_ref.shape[1] // 3
    query = local_ref[:, pl.ds(0, rows)].reshape(slots * rows, HEAD_DIM)
    for copy in range(query_ref.shape[0]):
        query_ref[copy] = query
    for place in range(2):
        block = local_ref[:, pl.ds((place + 1) * rows, rows)]
        key_value_ref[place] = block.reshape(slots * rows, HEAD_DIM)


def attend_kernel(q_ref, key_value_ref, out_ref):
    groups, tokens, width = q_ref.shape
    count = key_value_ref.shape[0] * tokens
    key = key_value_ref[:, 0].reshape(count, width)
    value = key_value_ref[:, 1].reshape(count, width)
    columns = []
    for group in range(0, groups, GROUP_STEP):
        query = q_ref[pl.ds(group, GROUP_STEP)].reshape(GROUP_STEP * tokens, width)
        score = lax.dot_general(
            query, key, (((1,), (1,)), ((), ())), preferred_element_type=jnp.float32
        )
        highest = jnp.max(score, axis=1, keepdims=True)
        expd = jnp.exp2((score - highest) * (SCALE * LOG2E))
        total = jnp.sum(expd, axis=1, keepdims=True)
        summed = jnp.dot(expd.astype(jnp.bfloat16), value, preferred_element_type=jnp.float32)
        for step in range(GROUP_STEP):
            rows = slice(step * tokens, (step + 1) * tokens)
            out_ref[group + step, pl.ds(0, tokens)] = summed[rows].astype(jnp.bfloat16)
            columns.append((highest[rows], total[rows]))
    for group, packed in enumerate(pack_stats(columns)):
        out_ref[group, pl.ds(tokens, STAT_ROWS)] = packed


def combine_kernel(part_ref, out_ref):
    groups = part_ref.shape[0]
    tokens = part_ref.shape[1] - STAT_ROWS
    copies, rows, _ = out_ref.shape
    stats = unpack_stats(part_ref[:, pl.ds(tokens, STAT_ROWS)], tokens)
    lane = lax.broadcasted_iota(jnp.int32, stats.shape, 1)
    is_maximum = (lane % STAT_LANES == 0) & (lane < groups * STAT_LANES)
    highest = jnp.max(jnp.where(is_maximum, stats, -jnp.inf), axis=1, keepdims=True)
    weight = jnp.where(is_maximum, jnp.exp2((stats - highest) * (SCALE * LOG2E)), 0.0)
    sums = jnp.where(is_maximum, pltpu.roll(stats, HEAD_DIM - 1, 1), 0.0)
    total = jnp.sum(weight * sums, axis=1, keepdims=True)
    summed = jnp.zeros(stats.shape, jnp.float32)
    for group in range(groups):
        at = group * STAT_LANES
        part = part_ref[group, pl.ds(0, tokens)].astype(jnp.float32)
        summed += part * weight[:, at : at + 1]
    attended = (summed / total).astype(jnp.bfloat16)
    repeats = copies * rows // tokens
    for block in range(tokens // rows):
        for repeat in range(repeats):
            out_ref[block * repeats + repeat] = attended[block * rows : (block + 1) * rows]


def mix_kernel(attended_ref, gate_ref, weight_ref, out_ref, held_ref, semaphores):
    heads = weight_ref.shape[0] // HEAD_DIM
    pieces = semaphores.shape[0]
    span = heads // pieces
    copies = []
    for piece in range(pieces):
        rows = pl.ds(piece * span * HEAD_DIM, span * HEAD_DIM)
        copy = pltpu.make_async_copy(weight_ref.at[rows], held_ref.at[rows], semaphores.at[piece])
        copy.start()
        copies.append(copy)
    product = jnp.zeros(out_ref.shape, jnp.float32)
    for piece, copy in enumerate(copies):
        first = piece * span
        block = jnp.concatenate(
            [attended_ref[head] for head in range(first, first + span)], axis=1
        )
        copy.wait()
        product += jnp.dot(
            block,
            held_ref[pl.ds(first * HEAD_DIM, span * HEAD_DIM)],
            preferred_element_type=jnp.float32,
        )
    out_ref[...] = (product * gate_ref[...][None, :]).astype(jnp.bfloat16)


def exchange(blocks, axes):
    return lax.all_to_all(blocks, axes, split_axis=0, concat_axis=0, tiled=True)


def on_device(queries, keys, vals, out_weight, gate):
    slots = lax.axis_size(HEAD_AXES)
    rows, width = queries.shape
    heads = width // HEAD_DIM
    tokens = slots * rows
    own_tokens = lax.axis_size("tp") * rows
    stacked = jnp.stack([queries, keys, vals], axis=0).reshape(3, rows, heads, HEAD_DIM)
    stacked = stacked.transpose(2, 0, 1, 3).reshape(heads, 3 * rows, HEAD_DIM)
    stacked = jnp.pad(stacked, ((0, slots - heads), (0, 0), (0, 0)))
    query_copies, own_key_value = pl.pallas_call(
        split_kernel,
        out_shape=[
            jax.ShapeDtypeStruct((lax.axis_size(QUERY_AXES), tokens, HEAD_DIM), jnp.bfloat16),
            jax.ShapeDtypeStruct((2, tokens, HEAD_DIM), jnp.bfloat16),
        ],
        in_specs=[IN_VMEM],
        out_specs=[IN_VMEM] * 2,
        compiler_params=pltpu.CompilerParams(vmem_limit_bytes=KERNEL_VMEM),
        name="split",
    )(exchange(stacked, HEAD_AXES))
    group = exchange(query_copies, QUERY_AXES)
    key_value = own_key_value[None]
    for pairs in KEY_PAIRS:
        key_value = lax.all_gather(
            key_value, KEY_AXIS, axis=0, tiled=True, axis_index_groups=pairs
        )
    key_value, group = lax.optimization_barrier((key_value, group))
    partial = pl.pallas_call(
        attend_kernel,
        out_shape=jax.ShapeDtypeStruct(
            (group.shape[0], tokens + STAT_ROWS, HEAD_DIM), jnp.bfloat16
        ),
        in_specs=[IN_VMEM] * 2,
        out_specs=IN_VMEM,
        compiler_params=pltpu.CompilerParams(vmem_limit_bytes=KERNEL_VMEM),
        name="attend",
    )(group, key_value)
    partial = exchange(partial, QUERY_AXES)
    attended = pl.pallas_call(
        combine_kernel,
        out_shape=jax.ShapeDtypeStruct((slots, own_tokens, HEAD_DIM), jnp.bfloat16),
        in_specs=[IN_VMEM],
        out_specs=IN_VMEM,
        compiler_params=pltpu.CompilerParams(vmem_limit_bytes=KERNEL_VMEM),
        name="combine",
    )(partial)
    attended = exchange(attended, HEAD_AXES)
    return pl.pallas_call(
        mix_kernel,
        out_shape=jax.ShapeDtypeStruct((own_tokens, out_weight.shape[1]), jnp.bfloat16),
        in_specs=[IN_VMEM, IN_VMEM, pl.BlockSpec(memory_space=pltpu.HBM)],
        out_specs=IN_VMEM,
        scratch_shapes=[
            pltpu.VMEM(out_weight.shape, out_weight.dtype),
            pltpu.SemaphoreType.DMA((heads // 2,)),
        ],
        compiler_params=pltpu.CompilerParams(vmem_limit_bytes=MIX_VMEM),
        name="mix",
    )(attended, gate, out_weight)


def solution(mesh):
    ctx = ("zl", "y", "x", "c")
    fine = Mesh(mesh.devices.reshape(3, 8, 4, 2, 4), (*ctx, "tp"))
    return jax.shard_map(
        on_device,
        mesh=fine,
        in_specs=(
            P((*ctx, "tp"), None),
            P((*ctx, "tp"), None),
            P((*ctx, "tp"), None),
            P(None, "tp"),
            P("tp"),
        ),
        out_specs=P(ctx, "tp"),
        check_vma=False,
    )
```

```python
import jax
import jax.numpy as jnp
from jax import lax
from jax.experimental import pallas as pl
from jax.experimental.pallas import tpu as pltpu
from jax.sharding import Mesh, PartitionSpec as P

HEAD_DIM = 128
LOG2E = 1.4426950408889634
SCALE = HEAD_DIM ** -0.5
HEAD_AXES = ("zl", "tp")
QUERY_AXES = ("y",)
KEY_AXES = ("x", "c")
STATS = 2
STAT_LANES = 8
STAT_ROWS = 16
GROUP_STEP = 4
KERNEL_VMEM = 16 * 1024 * 1024
MIX_VMEM = 50 * 1024 * 1024
IN_VMEM = pl.BlockSpec(memory_space=pltpu.VMEM)


def pack_stats(columns):
    tokens = columns[0][0].shape[0]
    lane = lax.broadcasted_iota(jnp.int32, (tokens, HEAD_DIM), 1)
    stats = jnp.zeros((tokens, HEAD_DIM), jnp.float32)
    for group, values in enumerate(columns):
        for place, value in enumerate(values):
            stats = jnp.where(lane == group * STAT_LANES + place, value, stats)
    high = stats.astype(jnp.bfloat16).astype(jnp.float32)
    rest = stats - high
    middle = rest.astype(jnp.bfloat16).astype(jnp.float32)
    low = rest - middle
    pieces = high + pltpu.roll(middle, STATS, 1) + pltpu.roll(low, 2 * STATS, 1)
    filler = jnp.zeros((2 * HEAD_DIM - tokens, HEAD_DIM), jnp.float32)
    rows = jnp.concatenate([pieces, filler], axis=0).T
    packed = []
    for group in range(len(columns)):
        own = rows[group * STAT_LANES : (group + 1) * STAT_LANES]
        both = jnp.concatenate([own[:, :HEAD_DIM], own[:, HEAD_DIM:]], axis=0)
        packed.append(both.astype(jnp.bfloat16))
    return packed


def unpack_stats(packed, tokens):
    groups = packed.shape[0]
    rows = packed.astype(jnp.float32)
    filler = jnp.zeros((HEAD_DIM - groups * STAT_LANES, HEAD_DIM), jnp.float32)
    halves = [
        jnp.concatenate(
            [rows[group, half : half + STAT_LANES] for group in range(groups)] + [filler], axis=0
        )
        for half in (0, STAT_LANES)
    ]
    pieces = jnp.concatenate([half.T for half in halves], axis=0)[:tokens]
    return (
        pieces
        + pltpu.roll(pieces, HEAD_DIM - STATS, 1)
        + pltpu.roll(pieces, HEAD_DIM - 2 * STATS, 1)
    )


def split_kernel(local_ref, query_ref, key_value_ref):
    slots = local_ref.shape[0]
    heads, tokens = key_value_ref.shape[1:3]
    rows = tokens // slots
    for head in range(heads):
        for place in range(3):
            span = pl.ds((head * 3 + place) * rows, rows)
            block = local_ref[:, span].reshape(tokens, HEAD_DIM)
            if place:
                key_value_ref[place - 1, head] = block
                continue
            for copy in range(query_ref.shape[0]):
                query_ref[copy, head] = block


def attend_kernel(q_ref, key_value_ref, out_ref):
    groups, heads, tokens, width = q_ref.shape
    count = key_value_ref.shape[0] * tokens
    columns = [[None] * heads for _ in range(groups)]
    for head in range(heads):
        key = key_value_ref[:, 0, head].reshape(count, width)
        value = key_value_ref[:, 1, head].reshape(count, width)
        for group in range(0, groups, GROUP_STEP):
            query = q_ref[pl.ds(group, GROUP_STEP), head].reshape(GROUP_STEP * tokens, width)
            score = lax.dot_general(
                query, key, (((1,), (1,)), ((), ())), preferred_element_type=jnp.float32
            )
            highest = jnp.max(score, axis=1, keepdims=True)
            expd = jnp.exp2((score - highest) * (SCALE * LOG2E))
            total = jnp.sum(expd, axis=1, keepdims=True)
            summed = jnp.dot(expd.astype(jnp.bfloat16), value, preferred_element_type=jnp.float32)
            for step in range(GROUP_STEP):
                rows = slice(step * tokens, (step + 1) * tokens)
                out_ref[group + step, pl.ds(head * tokens, tokens)] = summed[rows].astype(
                    jnp.bfloat16
                )
                columns[group + step][head] = (highest[rows], total[rows])
    columns = [
        [jnp.concatenate(values, axis=0) for values in zip(*by_head)] for by_head in columns
    ]
    for group, packed in enumerate(pack_stats(columns)):
        out_ref[group, pl.ds(heads * tokens, STAT_ROWS)] = packed


def combine_kernel(part_ref, out_ref):
    groups = part_ref.shape[0]
    tokens = part_ref.shape[1] - STAT_ROWS
    slots, heads, rows, _ = out_ref.shape
    stats = unpack_stats(part_ref[:, pl.ds(tokens, STAT_ROWS)], tokens)
    lane = lax.broadcasted_iota(jnp.int32, stats.shape, 1)
    is_maximum = (lane % STAT_LANES == 0) & (lane < groups * STAT_LANES)
    highest = jnp.max(jnp.where(is_maximum, stats, -jnp.inf), axis=1, keepdims=True)
    weight = jnp.where(is_maximum, jnp.exp2((stats - highest) * (SCALE * LOG2E)), 0.0)
    sums = jnp.where(is_maximum, pltpu.roll(stats, HEAD_DIM - 1, 1), 0.0)
    total = jnp.sum(weight * sums, axis=1, keepdims=True)
    summed = jnp.zeros(stats.shape, jnp.float32)
    for group in range(groups):
        at = group * STAT_LANES
        part = part_ref[group, pl.ds(0, tokens)].astype(jnp.float32)
        summed += part * weight[:, at : at + 1]
    attended = (summed / total).astype(jnp.bfloat16)
    blocks = tokens // heads // rows
    for slot in range(slots):
        for head in range(heads):
            start = (head * blocks + slot * blocks // slots) * rows
            out_ref[slot, head] = attended[start : start + rows]


def mix_kernel(attended_ref, gate_ref, weight_ref, out_ref, held_ref, semaphores):
    held = attended_ref.shape[1]
    heads = weight_ref.shape[0] // HEAD_DIM
    pieces = semaphores.shape[0]
    span = heads // pieces
    copies = []
    for piece in range(pieces):
        rows = pl.ds(piece * span * HEAD_DIM, span * HEAD_DIM)
        copy = pltpu.make_async_copy(weight_ref.at[rows], held_ref.at[rows], semaphores.at[piece])
        copy.start()
        copies.append(copy)
    product = jnp.zeros(out_ref.shape, jnp.float32)
    for piece, copy in enumerate(copies):
        first = piece * span
        block = jnp.concatenate(
            [attended_ref[head // held, head % held] for head in range(first, first + span)],
            axis=1,
        )
        copy.wait()
        product += jnp.dot(
            block,
            held_ref[pl.ds(first * HEAD_DIM, span * HEAD_DIM)],
            preferred_element_type=jnp.float32,
        )
    out_ref[...] = (product * gate_ref[...][None, :]).astype(jnp.bfloat16)


def exchange(blocks, axes):
    return lax.all_to_all(blocks, axes, split_axis=0, concat_axis=0, tiled=True)


def on_device(queries, keys, vals, out_weight, gate):
    slots = lax.axis_size(HEAD_AXES)
    rows, width = queries.shape
    heads = width // HEAD_DIM
    held = -(-heads // slots)
    tokens = slots * rows
    own_tokens = lax.axis_size("tp") * rows
    stacked = jnp.stack([queries, keys, vals], axis=0).reshape(3, rows, heads, HEAD_DIM)
    stacked = stacked.transpose(2, 0, 1, 3).reshape(heads, 3 * rows, HEAD_DIM)
    stacked = jnp.pad(stacked, ((0, slots * held - heads), (0, 0), (0, 0)))
    stacked = stacked.reshape(slots, held * 3 * rows, HEAD_DIM)
    query_copies, own_key_value = pl.pallas_call(
        split_kernel,
        out_shape=[
            jax.ShapeDtypeStruct(
                (lax.axis_size(QUERY_AXES), held, tokens, HEAD_DIM), jnp.bfloat16
            ),
            jax.ShapeDtypeStruct((2, held, tokens, HEAD_DIM), jnp.bfloat16),
        ],
        in_specs=[IN_VMEM],
        out_specs=[IN_VMEM] * 2,
        compiler_params=pltpu.CompilerParams(vmem_limit_bytes=KERNEL_VMEM),
        name="split",
    )(exchange(stacked, HEAD_AXES))
    group = exchange(query_copies, QUERY_AXES)
    key_value = lax.all_gather(own_key_value, KEY_AXES, axis=0, tiled=False)
    key_value, group = lax.optimization_barrier((key_value, group))
    partial = pl.pallas_call(
        attend_kernel,
        out_shape=jax.ShapeDtypeStruct(
            (group.shape[0], held * tokens + STAT_ROWS, HEAD_DIM), jnp.bfloat16
        ),
        in_specs=[IN_VMEM] * 2,
        out_specs=IN_VMEM,
        compiler_params=pltpu.CompilerParams(vmem_limit_bytes=KERNEL_VMEM),
        name="attend",
    )(group, key_value)
    partial = exchange(partial, QUERY_AXES)
    attended = pl.pallas_call(
        combine_kernel,
        out_shape=jax.ShapeDtypeStruct((slots, held, own_tokens, HEAD_DIM), jnp.bfloat16),
        in_specs=[IN_VMEM],
        out_specs=IN_VMEM,
        compiler_params=pltpu.CompilerParams(vmem_limit_bytes=KERNEL_VMEM),
        name="combine",
    )(partial)
    attended = exchange(attended, HEAD_AXES)
    return pl.pallas_call(
        mix_kernel,
        out_shape=jax.ShapeDtypeStruct((own_tokens, out_weight.shape[1]), jnp.bfloat16),
        in_specs=[IN_VMEM, IN_VMEM, pl.BlockSpec(memory_space=pltpu.HBM)],
        out_specs=IN_VMEM,
        scratch_shapes=[
            pltpu.VMEM(out_weight.shape, out_weight.dtype),
            pltpu.SemaphoreType.DMA((heads // 2,)),
        ],
        compiler_params=pltpu.CompilerParams(vmem_limit_bytes=MIX_VMEM),
        name="mix",
    )(attended, gate, out_weight)


def solution(mesh):
    ctx = ("zl", "y", "x", "c")
    fine = Mesh(mesh.devices.reshape(3, 8, 4, 2, 4), (*ctx, "tp"))
    return jax.shard_map(
        on_device,
        mesh=fine,
        in_specs=(
            P((*ctx, "tp"), None),
            P((*ctx, "tp"), None),
            P((*ctx, "tp"), None),
            P(None, "tp"),
            P("tp"),
        ),
        out_specs=P(ctx, "tp"),
        check_vma=False,
    )
```

```python
import jax
import jax.numpy as jnp
from jax import lax
from jax.experimental import pallas as pl
from jax.experimental.pallas import tpu as pltpu
from jax.sharding import Mesh, PartitionSpec as P

HEAD_DIM = 128
LOG2E = 1.4426950408889634
SCALE = HEAD_DIM ** -0.5
HEAD_AXES = ("zl", "c", "tp")
QUERY_AXES = ("y",)
KEY_AXES = ("x",)
STATS = 2
STAT_LANES = 8
STAT_ROWS = 16
GROUP_STEP = 2
EARLY_HEADS = 10
KERNEL_VMEM = 16 * 1024 * 1024
MIX_VMEM = 50 * 1024 * 1024
IN_VMEM = pl.BlockSpec(memory_space=pltpu.VMEM)


def pack_stats(columns):
    tokens = columns[0][0].shape[0]
    lane = lax.broadcasted_iota(jnp.int32, (tokens, HEAD_DIM), 1)
    stats = jnp.zeros((tokens, HEAD_DIM), jnp.float32)
    for group, values in enumerate(columns):
        for place, value in enumerate(values):
            stats = jnp.where(lane == group * STAT_LANES + place, value, stats)
    high = stats.astype(jnp.bfloat16).astype(jnp.float32)
    rest = stats - high
    middle = rest.astype(jnp.bfloat16).astype(jnp.float32)
    low = rest - middle
    pieces = high + pltpu.roll(middle, STATS, 1) + pltpu.roll(low, 2 * STATS, 1)
    filler = jnp.zeros((2 * HEAD_DIM - tokens, HEAD_DIM), jnp.float32)
    rows = jnp.concatenate([pieces, filler], axis=0).T
    packed = []
    for group in range(len(columns)):
        own = rows[group * STAT_LANES : (group + 1) * STAT_LANES]
        both = jnp.concatenate([own[:, :HEAD_DIM], own[:, HEAD_DIM:]], axis=0)
        packed.append(both.astype(jnp.bfloat16))
    return packed


def unpack_stats(packed, tokens):
    groups = packed.shape[0]
    rows = packed.astype(jnp.float32)
    filler = jnp.zeros((HEAD_DIM - groups * STAT_LANES, HEAD_DIM), jnp.float32)
    halves = [
        jnp.concatenate(
            [rows[group, half : half + STAT_LANES] for group in range(groups)] + [filler], axis=0
        )
        for half in (0, STAT_LANES)
    ]
    pieces = jnp.concatenate([half.T for half in halves], axis=0)[:tokens]
    return (
        pieces
        + pltpu.roll(pieces, HEAD_DIM - STATS, 1)
        + pltpu.roll(pieces, HEAD_DIM - 2 * STATS, 1)
    )


def split_kernel(local_ref, query_ref, key_value_ref):
    slots = local_ref.shape[0]
    rows = local_ref.shape[1] // 3
    query = local_ref[:, pl.ds(0, rows)].reshape(slots * rows, HEAD_DIM)
    for copy in range(query_ref.shape[0]):
        query_ref[copy] = query
    for place in range(2):
        block = local_ref[:, pl.ds((place + 1) * rows, rows)]
        key_value_ref[place] = block.reshape(slots * rows, HEAD_DIM)


def attend_kernel(q_ref, key_value_ref, out_ref):
    groups, tokens, width = q_ref.shape
    count = key_value_ref.shape[0] * tokens
    key = key_value_ref[:, 0].reshape(count, width)
    value = key_value_ref[:, 1].reshape(count, width)
    columns = []
    for group in range(0, groups, GROUP_STEP):
        query = q_ref[pl.ds(group, GROUP_STEP)].reshape(GROUP_STEP * tokens, width)
        score = lax.dot_general(
            query, key, (((1,), (1,)), ((), ())), preferred_element_type=jnp.float32
        )
        highest = jnp.max(score, axis=1, keepdims=True)
        expd = jnp.exp2((score - highest) * (SCALE * LOG2E))
        total = jnp.sum(expd, axis=1, keepdims=True)
        summed = jnp.dot(expd.astype(jnp.bfloat16), value, preferred_element_type=jnp.float32)
        for step in range(GROUP_STEP):
            rows = slice(step * tokens, (step + 1) * tokens)
            out_ref[group + step, pl.ds(0, tokens)] = summed[rows].astype(jnp.bfloat16)
            columns.append((highest[rows], total[rows]))
    for group, packed in enumerate(pack_stats(columns)):
        out_ref[group, pl.ds(tokens, STAT_ROWS)] = packed


def combine_kernel(part_ref, out_ref):
    groups = part_ref.shape[0]
    tokens = part_ref.shape[1] - STAT_ROWS
    copies, rows, _ = out_ref.shape
    stats = unpack_stats(part_ref[:, pl.ds(tokens, STAT_ROWS)], tokens)
    lane = lax.broadcasted_iota(jnp.int32, stats.shape, 1)
    is_maximum = (lane % STAT_LANES == 0) & (lane < groups * STAT_LANES)
    highest = jnp.max(jnp.where(is_maximum, stats, -jnp.inf), axis=1, keepdims=True)
    weight = jnp.where(is_maximum, jnp.exp2((stats - highest) * (SCALE * LOG2E)), 0.0)
    sums = jnp.where(is_maximum, pltpu.roll(stats, HEAD_DIM - 1, 1), 0.0)
    total = jnp.sum(weight * sums, axis=1, keepdims=True)
    summed = jnp.zeros(stats.shape, jnp.float32)
    for group in range(groups):
        at = group * STAT_LANES
        part = part_ref[group, pl.ds(0, tokens)].astype(jnp.float32)
        summed += part * weight[:, at : at + 1]
    attended = (summed / total).astype(jnp.bfloat16)
    repeats = copies * rows // tokens
    for block in range(tokens // rows):
        for repeat in range(repeats):
            out_ref[block * repeats + repeat] = attended[block * rows : (block + 1) * rows]


def load_rows(weight_ref, held_ref, semaphores, first):
    rows = held_ref.shape[0] // semaphores.shape[0]
    copies = []
    for piece in range(semaphores.shape[0]):
        copy = pltpu.make_async_copy(
            weight_ref.at[pl.ds(first + piece * rows, rows)],
            held_ref.at[pl.ds(piece * rows, rows)],
            semaphores.at[piece],
        )
        copy.start()
        copies.append(copy)
    return copies


def fetch_kernel(weight_ref, gate_ref, held_ref, row_ref, semaphores):
    copies = load_rows(weight_ref, held_ref, semaphores, 0)
    row_ref[...] = gate_ref[...][None, :]
    for copy in copies:
        copy.wait()


def mix_kernel(attended_ref, row_ref, first_ref, weight_ref, out_ref, held_ref, semaphores):
    early = first_ref.shape[0] // HEAD_DIM
    copies = load_rows(weight_ref, held_ref, semaphores, first_ref.shape[0])
    span = held_ref.shape[0] // HEAD_DIM // len(copies)

    def product_of(first, count, rows):
        block = jnp.concatenate(
            [attended_ref[head] for head in range(first, first + count)], axis=1
        )
        return jnp.dot(block, rows, preferred_element_type=jnp.float32)

    product = product_of(0, early, first_ref[...])
    for piece, copy in enumerate(copies):
        copy.wait()
        rows = held_ref[pl.ds(piece * span * HEAD_DIM, span * HEAD_DIM)]
        product += product_of(early + piece * span, span, rows)
    out_ref[...] = (product * row_ref[...]).astype(jnp.bfloat16)


def exchange(blocks, axes):
    return lax.all_to_all(blocks, axes, split_axis=0, concat_axis=0, tiled=True)


def on_device(queries, keys, vals, out_weight, gate):
    slots = lax.axis_size(HEAD_AXES)
    rows, width = queries.shape
    heads = width // HEAD_DIM
    tokens = slots * rows
    own_tokens = lax.axis_size("tp") * rows
    stacked = jnp.stack([queries, keys, vals], axis=0).reshape(3, rows, heads, HEAD_DIM)
    stacked = stacked.transpose(2, 0, 1, 3).reshape(heads, 3 * rows, HEAD_DIM)
    stacked = jnp.pad(stacked, ((0, slots - heads), (0, 0), (0, 0)))
    query_copies, own_key_value = pl.pallas_call(
        split_kernel,
        out_shape=[
            jax.ShapeDtypeStruct((lax.axis_size(QUERY_AXES), tokens, HEAD_DIM), jnp.bfloat16),
            jax.ShapeDtypeStruct((2, tokens, HEAD_DIM), jnp.bfloat16),
        ],
        in_specs=[IN_VMEM],
        out_specs=[IN_VMEM] * 2,
        compiler_params=pltpu.CompilerParams(vmem_limit_bytes=KERNEL_VMEM),
        name="split",
    )(exchange(stacked, HEAD_AXES))
    group = exchange(query_copies, QUERY_AXES)
    key_value = lax.all_gather(own_key_value, KEY_AXES, axis=0, tiled=False)
    key_value, group = lax.optimization_barrier((key_value, group))
    partial = pl.pallas_call(
        attend_kernel,
        out_shape=jax.ShapeDtypeStruct(
            (group.shape[0], tokens + STAT_ROWS, HEAD_DIM), jnp.bfloat16
        ),
        in_specs=[IN_VMEM] * 2,
        out_specs=IN_VMEM,
        compiler_params=pltpu.CompilerParams(vmem_limit_bytes=KERNEL_VMEM),
        name="attend",
    )(group, key_value)
    partial = exchange(partial, QUERY_AXES)
    attended = pl.pallas_call(
        combine_kernel,
        out_shape=jax.ShapeDtypeStruct((slots, own_tokens, HEAD_DIM), jnp.bfloat16),
        in_specs=[IN_VMEM],
        out_specs=IN_VMEM,
        compiler_params=pltpu.CompilerParams(vmem_limit_bytes=KERNEL_VMEM),
        name="combine",
    )(partial)
    channels = out_weight.shape[1]
    attended, weight = lax.optimization_barrier((attended, out_weight))
    in_hbm = pl.BlockSpec(memory_space=pltpu.HBM)
    first, row = pl.pallas_call(
        fetch_kernel,
        out_shape=[
            jax.ShapeDtypeStruct((EARLY_HEADS * HEAD_DIM, channels), weight.dtype),
            jax.ShapeDtypeStruct((1, channels), gate.dtype),
        ],
        in_specs=[in_hbm, IN_VMEM],
        out_specs=[IN_VMEM] * 2,
        scratch_shapes=[pltpu.SemaphoreType.DMA((EARLY_HEADS // 2,))],
        compiler_params=pltpu.CompilerParams(vmem_limit_bytes=MIX_VMEM),
        cost_estimate=pl.CostEstimate(
            flops=0, bytes_accessed=4 * EARLY_HEADS * HEAD_DIM * channels, transcendentals=0
        ),
        name="fetch",
    )(weight, gate)
    attended = exchange(attended, HEAD_AXES)
    attended, first, row = lax.optimization_barrier((attended, first, row))
    late = heads - EARLY_HEADS
    return pl.pallas_call(
        mix_kernel,
        out_shape=jax.ShapeDtypeStruct((own_tokens, channels), jnp.bfloat16),
        in_specs=[IN_VMEM, IN_VMEM, IN_VMEM, in_hbm],
        out_specs=IN_VMEM,
        scratch_shapes=[
            pltpu.VMEM((late * HEAD_DIM, channels), out_weight.dtype),
            pltpu.SemaphoreType.DMA((late // 2,)),
        ],
        compiler_params=pltpu.CompilerParams(vmem_limit_bytes=MIX_VMEM),
        name="mix",
    )(attended, row, first, weight)


def solution(mesh):
    ctx = ("zl", "y", "x", "c")
    fine = Mesh(mesh.devices.reshape(3, 8, 4, 2, 4), (*ctx, "tp"))
    return jax.shard_map(
        on_device,
        mesh=fine,
        in_specs=(
            P((*ctx, "tp"), None),
            P((*ctx, "tp"), None),
            P((*ctx, "tp"), None),
            P(None, "tp"),
            P("tp"),
        ),
        out_specs=P(ctx, "tp"),
        check_vma=False,
    )
```

```python
import jax
import jax.numpy as jnp
from jax import lax
from jax.experimental import pallas as pl
from jax.experimental.pallas import tpu as pltpu
from jax.sharding import Mesh, PartitionSpec as P

HEAD_DIM = 128
LOG2E = 1.4426950408889634
SCALE = HEAD_DIM ** -0.5
HEAD_AXES = ("zl", "c", "tp")
QUERY_AXES = ("x",)
KEY_AXES = ("y",)
STATS = 2
STAT_LANES = 8
STAT_ROWS = 16
GROUP_STEP = 1
EARLY_HEADS = 10
KERNEL_VMEM = 16 * 1024 * 1024
MIX_VMEM = 50 * 1024 * 1024
IN_VMEM = pl.BlockSpec(memory_space=pltpu.VMEM)


def pack_stats(columns):
    tokens = columns[0][0].shape[0]
    lane = lax.broadcasted_iota(jnp.int32, (tokens, HEAD_DIM), 1)
    stats = jnp.zeros((tokens, HEAD_DIM), jnp.float32)
    for group, values in enumerate(columns):
        for place, value in enumerate(values):
            stats = jnp.where(lane == group * STAT_LANES + place, value, stats)
    high = stats.astype(jnp.bfloat16).astype(jnp.float32)
    rest = stats - high
    middle = rest.astype(jnp.bfloat16).astype(jnp.float32)
    low = rest - middle
    pieces = high + pltpu.roll(middle, STATS, 1) + pltpu.roll(low, 2 * STATS, 1)
    filler = jnp.zeros((2 * HEAD_DIM - tokens, HEAD_DIM), jnp.float32)
    rows = jnp.concatenate([pieces, filler], axis=0).T
    packed = []
    for group in range(len(columns)):
        own = rows[group * STAT_LANES : (group + 1) * STAT_LANES]
        both = jnp.concatenate([own[:, :HEAD_DIM], own[:, HEAD_DIM:]], axis=0)
        packed.append(both.astype(jnp.bfloat16))
    return packed


def unpack_stats(packed, tokens):
    groups = packed.shape[0]
    rows = packed.astype(jnp.float32)
    filler = jnp.zeros((HEAD_DIM - groups * STAT_LANES, HEAD_DIM), jnp.float32)
    halves = [
        jnp.concatenate(
            [rows[group, half : half + STAT_LANES] for group in range(groups)] + [filler], axis=0
        )
        for half in (0, STAT_LANES)
    ]
    pieces = jnp.concatenate([half.T for half in halves], axis=0)[:tokens]
    return (
        pieces
        + pltpu.roll(pieces, HEAD_DIM - STATS, 1)
        + pltpu.roll(pieces, HEAD_DIM - 2 * STATS, 1)
    )


def split_kernel(local_ref, query_ref, key_value_ref):
    slots = local_ref.shape[0]
    rows = local_ref.shape[1] // 3
    query_ref[...] = local_ref[:, pl.ds(0, rows)].reshape(slots * rows, HEAD_DIM)
    for place in range(2):
        block = local_ref[:, pl.ds((place + 1) * rows, rows)].reshape(slots * rows, HEAD_DIM)
        for copy in range(key_value_ref.shape[0]):
            key_value_ref[copy, place] = block


def attend_kernel(q_ref, key_value_ref, out_ref):
    groups, tokens, width = q_ref.shape
    count = key_value_ref.shape[0] * tokens
    key = key_value_ref[:, 0].reshape(count, width)
    value = key_value_ref[:, 1].reshape(count, width)
    columns = []
    for group in range(0, groups, GROUP_STEP):
        query = q_ref[pl.ds(group, GROUP_STEP)].reshape(GROUP_STEP * tokens, width)
        score = lax.dot_general(
            query, key, (((1,), (1,)), ((), ())), preferred_element_type=jnp.float32
        )
        highest = jnp.max(score, axis=1, keepdims=True)
        expd = jnp.exp2((score - highest) * (SCALE * LOG2E))
        total = jnp.sum(expd, axis=1, keepdims=True)
        summed = jnp.dot(expd.astype(jnp.bfloat16), value, preferred_element_type=jnp.float32)
        for step in range(GROUP_STEP):
            rows = slice(step * tokens, (step + 1) * tokens)
            out_ref[group + step, pl.ds(0, tokens)] = summed[rows].astype(jnp.bfloat16)
            columns.append((highest[rows], total[rows]))
    for group, packed in enumerate(pack_stats(columns)):
        out_ref[group, pl.ds(tokens, STAT_ROWS)] = packed


def combine_kernel(part_ref, out_ref):
    groups = part_ref.shape[0]
    tokens = part_ref.shape[1] - STAT_ROWS
    copies, rows, _ = out_ref.shape
    stats = unpack_stats(part_ref[:, pl.ds(tokens, STAT_ROWS)], tokens)
    lane = lax.broadcasted_iota(jnp.int32, stats.shape, 1)
    is_maximum = (lane % STAT_LANES == 0) & (lane < groups * STAT_LANES)
    highest = jnp.max(jnp.where(is_maximum, stats, -jnp.inf), axis=1, keepdims=True)
    weight = jnp.where(is_maximum, jnp.exp2((stats - highest) * (SCALE * LOG2E)), 0.0)
    sums = jnp.where(is_maximum, pltpu.roll(stats, HEAD_DIM - 1, 1), 0.0)
    total = jnp.sum(weight * sums, axis=1, keepdims=True)
    summed = jnp.zeros(stats.shape, jnp.float32)
    for group in range(groups):
        at = group * STAT_LANES
        part = part_ref[group, pl.ds(0, tokens)].astype(jnp.float32)
        summed += part * weight[:, at : at + 1]
    attended = (summed / total).astype(jnp.bfloat16)
    repeats = copies * rows // tokens
    for block in range(tokens // rows):
        for repeat in range(repeats):
            out_ref[block * repeats + repeat] = attended[block * rows : (block + 1) * rows]


def load_rows(weight_ref, held_ref, semaphores, first):
    rows = held_ref.shape[0] // semaphores.shape[0]
    copies = []
    for piece in range(semaphores.shape[0]):
        copy = pltpu.make_async_copy(
            weight_ref.at[pl.ds(first + piece * rows, rows)],
            held_ref.at[pl.ds(piece * rows, rows)],
            semaphores.at[piece],
        )
        copy.start()
        copies.append(copy)
    return copies


def fetch_kernel(weight_ref, gate_ref, held_ref, row_ref, semaphores):
    copies = load_rows(weight_ref, held_ref, semaphores, 0)
    row_ref[...] = gate_ref[...][None, :]
    for copy in copies:
        copy.wait()


def mix_kernel(attended_ref, row_ref, first_ref, weight_ref, out_ref, held_ref, semaphores):
    early = first_ref.shape[0] // HEAD_DIM
    copies = load_rows(weight_ref, held_ref, semaphores, first_ref.shape[0])
    span = held_ref.shape[0] // HEAD_DIM // len(copies)

    def product_of(first, count, rows):
        block = jnp.concatenate(
            [attended_ref[head] for head in range(first, first + count)], axis=1
        )
        return jnp.dot(block, rows, preferred_element_type=jnp.float32)

    product = product_of(0, early, first_ref[...])
    for piece, copy in enumerate(copies):
        copy.wait()
        rows = held_ref[pl.ds(piece * span * HEAD_DIM, span * HEAD_DIM)]
        product += product_of(early + piece * span, span, rows)
    out_ref[...] = (product * row_ref[...]).astype(jnp.bfloat16)


def exchange(blocks, axes):
    return lax.all_to_all(blocks, axes, split_axis=0, concat_axis=0, tiled=True)


def on_device(queries, keys, vals, out_weight, gate):
    slots = lax.axis_size(HEAD_AXES)
    rows, width = queries.shape
    heads = width // HEAD_DIM
    tokens = slots * rows
    own_tokens = lax.axis_size("tp") * rows
    stacked = jnp.stack([queries, keys, vals], axis=0).reshape(3, rows, heads, HEAD_DIM)
    stacked = stacked.transpose(2, 0, 1, 3).reshape(heads, 3 * rows, HEAD_DIM)
    stacked = jnp.pad(stacked, ((0, slots - heads), (0, 0), (0, 0)))
    own_query, key_value_copies = pl.pallas_call(
        split_kernel,
        out_shape=[
            jax.ShapeDtypeStruct((tokens, HEAD_DIM), jnp.bfloat16),
            jax.ShapeDtypeStruct((lax.axis_size(KEY_AXES), 2, tokens, HEAD_DIM), jnp.bfloat16),
        ],
        in_specs=[IN_VMEM],
        out_specs=[IN_VMEM] * 2,
        compiler_params=pltpu.CompilerParams(vmem_limit_bytes=KERNEL_VMEM),
        name="split",
    )(exchange(stacked, HEAD_AXES))
    key_value = exchange(key_value_copies, KEY_AXES)
    group = lax.all_gather(own_query, QUERY_AXES, axis=0, tiled=False)
    key_value, group = lax.optimization_barrier((key_value, group))
    partial = pl.pallas_call(
        attend_kernel,
        out_shape=jax.ShapeDtypeStruct(
            (group.shape[0], tokens + STAT_ROWS, HEAD_DIM), jnp.bfloat16
        ),
        in_specs=[IN_VMEM] * 2,
        out_specs=IN_VMEM,
        compiler_params=pltpu.CompilerParams(vmem_limit_bytes=KERNEL_VMEM),
        name="attend",
    )(group, key_value)
    partial = exchange(partial, QUERY_AXES)
    attended = pl.pallas_call(
        combine_kernel,
        out_shape=jax.ShapeDtypeStruct((slots, own_tokens, HEAD_DIM), jnp.bfloat16),
        in_specs=[IN_VMEM],
        out_specs=IN_VMEM,
        compiler_params=pltpu.CompilerParams(vmem_limit_bytes=KERNEL_VMEM),
        name="combine",
    )(partial)
    channels = out_weight.shape[1]
    attended, weight = lax.optimization_barrier((attended, out_weight))
    in_hbm = pl.BlockSpec(memory_space=pltpu.HBM)
    first, row = pl.pallas_call(
        fetch_kernel,
        out_shape=[
            jax.ShapeDtypeStruct((EARLY_HEADS * HEAD_DIM, channels), weight.dtype),
            jax.ShapeDtypeStruct((1, channels), gate.dtype),
        ],
        in_specs=[in_hbm, IN_VMEM],
        out_specs=[IN_VMEM] * 2,
        scratch_shapes=[pltpu.SemaphoreType.DMA((EARLY_HEADS // 2,))],
        compiler_params=pltpu.CompilerParams(vmem_limit_bytes=MIX_VMEM),
        cost_estimate=pl.CostEstimate(
            flops=0, bytes_accessed=4 * EARLY_HEADS * HEAD_DIM * channels, transcendentals=0
        ),
        name="fetch",
    )(weight, gate)
    attended = exchange(attended, HEAD_AXES)
    attended, first, row = lax.optimization_barrier((attended, first, row))
    late = heads - EARLY_HEADS
    return pl.pallas_call(
        mix_kernel,
        out_shape=jax.ShapeDtypeStruct((own_tokens, channels), jnp.bfloat16),
        in_specs=[IN_VMEM, IN_VMEM, IN_VMEM, in_hbm],
        out_specs=IN_VMEM,
        scratch_shapes=[
            pltpu.VMEM((late * HEAD_DIM, channels), out_weight.dtype),
            pltpu.SemaphoreType.DMA((late // 2,)),
        ],
        compiler_params=pltpu.CompilerParams(vmem_limit_bytes=MIX_VMEM),
        name="mix",
    )(attended, row, first, weight)


def solution(mesh):
    ctx = ("zl", "y", "x", "c")
    fine = Mesh(mesh.devices.reshape(3, 8, 4, 2, 4), (*ctx, "tp"))
    return jax.shard_map(
        on_device,
        mesh=fine,
        in_specs=(
            P((*ctx, "tp"), None),
            P((*ctx, "tp"), None),
            P((*ctx, "tp"), None),
            P(None, "tp"),
            P("tp"),
        ),
        out_specs=P(ctx, "tp"),
        check_vma=False,
    )
```

```python
import jax
import jax.numpy as jnp
from jax import lax
from jax.experimental import pallas as pl
from jax.experimental.pallas import tpu as pltpu
from jax.sharding import Mesh, PartitionSpec as P

HEAD_DIM = 128
LOG2E = 1.4426950408889634
SCALE = HEAD_DIM ** -0.5
HEAD_AXES = ("zl", "c", "tp")
QUERY_AXES = ("x",)
KEY_AXES = ("y",)
STATS = 2
STAT_LANES = 8
STAT_ROWS = 16
GROUP_STEP = 1
EARLY_HEADS = 6
KERNEL_VMEM = 16 * 1024 * 1024
MIX_VMEM = 50 * 1024 * 1024
IN_VMEM = pl.BlockSpec(memory_space=pltpu.VMEM)


def pack_stats(columns):
    tokens = columns[0][0].shape[0]
    lane = lax.broadcasted_iota(jnp.int32, (tokens, HEAD_DIM), 1)
    stats = jnp.zeros((tokens, HEAD_DIM), jnp.float32)
    for group, values in enumerate(columns):
        for place, value in enumerate(values):
            stats = jnp.where(lane == group * STAT_LANES + place, value, stats)
    high = stats.astype(jnp.bfloat16).astype(jnp.float32)
    rest = stats - high
    middle = rest.astype(jnp.bfloat16).astype(jnp.float32)
    low = rest - middle
    pieces = high + pltpu.roll(middle, STATS, 1) + pltpu.roll(low, 2 * STATS, 1)
    filler = jnp.zeros((2 * HEAD_DIM - tokens, HEAD_DIM), jnp.float32)
    rows = jnp.concatenate([pieces, filler], axis=0).T
    packed = []
    for group in range(len(columns)):
        own = rows[group * STAT_LANES : (group + 1) * STAT_LANES]
        both = jnp.concatenate([own[:, :HEAD_DIM], own[:, HEAD_DIM:]], axis=0)
        packed.append(both.astype(jnp.bfloat16))
    return packed


def unpack_stats(packed, tokens):
    groups = packed.shape[0]
    rows = packed.astype(jnp.float32)
    filler = jnp.zeros((HEAD_DIM - groups * STAT_LANES, HEAD_DIM), jnp.float32)
    halves = [
        jnp.concatenate(
            [rows[group, half : half + STAT_LANES] for group in range(groups)] + [filler], axis=0
        )
        for half in (0, STAT_LANES)
    ]
    pieces = jnp.concatenate([half.T for half in halves], axis=0)[:tokens]
    return (
        pieces
        + pltpu.roll(pieces, HEAD_DIM - STATS, 1)
        + pltpu.roll(pieces, HEAD_DIM - 2 * STATS, 1)
    )


def split_kernel(local_ref, query_ref, key_value_ref):
    slots = local_ref.shape[0]
    rows = local_ref.shape[1] // 3
    query_ref[...] = local_ref[:, pl.ds(0, rows)].reshape(slots * rows, HEAD_DIM)
    for place in range(2):
        block = local_ref[:, pl.ds((place + 1) * rows, rows)].reshape(slots * rows, HEAD_DIM)
        for copy in range(key_value_ref.shape[0]):
            key_value_ref[copy, place] = block


def attend_kernel(q_ref, key_value_ref, out_ref):
    groups, tokens, width = q_ref.shape
    count = key_value_ref.shape[0] * tokens
    key = key_value_ref[:, 0].reshape(count, width)
    value = key_value_ref[:, 1].reshape(count, width)
    columns = []
    for group in range(0, groups, GROUP_STEP):
        query = q_ref[pl.ds(group, GROUP_STEP)].reshape(GROUP_STEP * tokens, width)
        score = lax.dot_general(
            query, key, (((1,), (1,)), ((), ())), preferred_element_type=jnp.float32
        )
        highest = jnp.max(score, axis=1, keepdims=True)
        expd = jnp.exp2((score - highest) * (SCALE * LOG2E))
        total = jnp.sum(expd, axis=1, keepdims=True)
        summed = jnp.dot(expd.astype(jnp.bfloat16), value, preferred_element_type=jnp.float32)
        for step in range(GROUP_STEP):
            rows = slice(step * tokens, (step + 1) * tokens)
            out_ref[group + step, pl.ds(0, tokens)] = summed[rows].astype(jnp.bfloat16)
            columns.append((highest[rows], total[rows]))
    for group, packed in enumerate(pack_stats(columns)):
        out_ref[group, pl.ds(tokens, STAT_ROWS)] = packed


def combine_kernel(part_ref, out_ref):
    groups = part_ref.shape[0]
    tokens = part_ref.shape[1] - STAT_ROWS
    copies, rows, _ = out_ref.shape
    stats = unpack_stats(part_ref[:, pl.ds(tokens, STAT_ROWS)], tokens)
    lane = lax.broadcasted_iota(jnp.int32, stats.shape, 1)
    is_maximum = (lane % STAT_LANES == 0) & (lane < groups * STAT_LANES)
    highest = jnp.max(jnp.where(is_maximum, stats, -jnp.inf), axis=1, keepdims=True)
    weight = jnp.where(is_maximum, jnp.exp2((stats - highest) * (SCALE * LOG2E)), 0.0)
    sums = jnp.where(is_maximum, pltpu.roll(stats, HEAD_DIM - 1, 1), 0.0)
    total = jnp.sum(weight * sums, axis=1, keepdims=True)
    summed = jnp.zeros(stats.shape, jnp.float32)
    for group in range(groups):
        at = group * STAT_LANES
        part = part_ref[group, pl.ds(0, tokens)].astype(jnp.float32)
        summed += part * weight[:, at : at + 1]
    attended = (summed / total).astype(jnp.bfloat16)
    repeats = copies * rows // tokens
    for block in range(tokens // rows):
        for repeat in range(repeats):
            out_ref[block * repeats + repeat] = attended[block * rows : (block + 1) * rows]


def load_rows(weight_ref, held_ref, semaphores, first):
    rows = held_ref.shape[0] // semaphores.shape[0]
    copies = []
    for piece in range(semaphores.shape[0]):
        copy = pltpu.make_async_copy(
            weight_ref.at[pl.ds(first + piece * rows, rows)],
            held_ref.at[pl.ds(piece * rows, rows)],
            semaphores.at[piece],
        )
        copy.start()
        copies.append(copy)
    return copies


def fetch_kernel(weight_ref, gate_ref, held_ref, row_ref, semaphores):
    copies = load_rows(weight_ref, held_ref, semaphores, 0)
    row_ref[...] = gate_ref[...][None, :]
    for copy in copies:
        copy.wait()


def mix_kernel(attended_ref, row_ref, first_ref, weight_ref, out_ref, held_ref, semaphores):
    early = first_ref.shape[0] // HEAD_DIM
    copies = load_rows(weight_ref, held_ref, semaphores, first_ref.shape[0])
    span = held_ref.shape[0] // HEAD_DIM // len(copies)

    def product_of(first, count, rows):
        block = jnp.concatenate(
            [attended_ref[head] for head in range(first, first + count)], axis=1
        )
        return jnp.dot(block, rows, preferred_element_type=jnp.float32)

    product = product_of(0, early, first_ref[...])
    for piece, copy in enumerate(copies):
        copy.wait()
        rows = held_ref[pl.ds(piece * span * HEAD_DIM, span * HEAD_DIM)]
        product += product_of(early + piece * span, span, rows)
    out_ref[...] = (product * row_ref[...]).astype(jnp.bfloat16)


def exchange(blocks, axes):
    return lax.all_to_all(blocks, axes, split_axis=0, concat_axis=0, tiled=True)


def on_device(queries, keys, vals, out_weight, gate):
    slots = lax.axis_size(HEAD_AXES)
    rows, width = queries.shape
    heads = width // HEAD_DIM
    tokens = slots * rows
    own_tokens = lax.axis_size("tp") * rows
    stacked = jnp.stack([queries, keys, vals], axis=0).reshape(3, rows, heads, HEAD_DIM)
    stacked = stacked.transpose(2, 0, 1, 3).reshape(heads, 3 * rows, HEAD_DIM)
    stacked = jnp.pad(stacked, ((0, slots - heads), (0, 0), (0, 0)))
    own_query, key_value_copies = pl.pallas_call(
        split_kernel,
        out_shape=[
            jax.ShapeDtypeStruct((tokens, HEAD_DIM), jnp.bfloat16),
            jax.ShapeDtypeStruct((lax.axis_size(KEY_AXES), 2, tokens, HEAD_DIM), jnp.bfloat16),
        ],
        in_specs=[IN_VMEM],
        out_specs=[IN_VMEM] * 2,
        compiler_params=pltpu.CompilerParams(vmem_limit_bytes=KERNEL_VMEM),
        name="split",
    )(exchange(stacked, HEAD_AXES))
    channels = out_weight.shape[1]
    key_value_copies, weight = lax.optimization_barrier((key_value_copies, out_weight))
    in_hbm = pl.BlockSpec(memory_space=pltpu.HBM)
    first, row = pl.pallas_call(
        fetch_kernel,
        out_shape=[
            jax.ShapeDtypeStruct((EARLY_HEADS * HEAD_DIM, channels), weight.dtype),
            jax.ShapeDtypeStruct((1, channels), gate.dtype),
        ],
        in_specs=[in_hbm, IN_VMEM],
        out_specs=[IN_VMEM] * 2,
        scratch_shapes=[pltpu.SemaphoreType.DMA((EARLY_HEADS // 2,))],
        compiler_params=pltpu.CompilerParams(vmem_limit_bytes=MIX_VMEM),
        cost_estimate=pl.CostEstimate(
            flops=0, bytes_accessed=4 * EARLY_HEADS * HEAD_DIM * channels, transcendentals=0
        ),
        name="fetch",
    )(weight, gate)
    key_value = exchange(key_value_copies, KEY_AXES)
    group = lax.all_gather(own_query, QUERY_AXES, axis=0, tiled=False)
    key_value, group, first, row = lax.optimization_barrier((key_value, group, first, row))
    partial = pl.pallas_call(
        attend_kernel,
        out_shape=jax.ShapeDtypeStruct(
            (group.shape[0], tokens + STAT_ROWS, HEAD_DIM), jnp.bfloat16
        ),
        in_specs=[IN_VMEM] * 2,
        out_specs=IN_VMEM,
        compiler_params=pltpu.CompilerParams(vmem_limit_bytes=KERNEL_VMEM),
        name="attend",
    )(group, key_value)
    partial = exchange(partial, QUERY_AXES)
    attended = pl.pallas_call(
        combine_kernel,
        out_shape=jax.ShapeDtypeStruct((slots, own_tokens, HEAD_DIM), jnp.bfloat16),
        in_specs=[IN_VMEM],
        out_specs=IN_VMEM,
        compiler_params=pltpu.CompilerParams(vmem_limit_bytes=KERNEL_VMEM),
        name="combine",
    )(partial)
    attended = exchange(attended, HEAD_AXES)
    late = heads - EARLY_HEADS
    return pl.pallas_call(
        mix_kernel,
        out_shape=jax.ShapeDtypeStruct((own_tokens, channels), jnp.bfloat16),
        in_specs=[IN_VMEM, IN_VMEM, IN_VMEM, in_hbm],
        out_specs=IN_VMEM,
        scratch_shapes=[
            pltpu.VMEM((late * HEAD_DIM, channels), out_weight.dtype),
            pltpu.SemaphoreType.DMA((late // 2,)),
        ],
        compiler_params=pltpu.CompilerParams(vmem_limit_bytes=MIX_VMEM),
        name="mix",
    )(attended, row, first, weight)


def solution(mesh):
    ctx = ("zl", "y", "x", "c")
    fine = Mesh(mesh.devices.reshape(3, 8, 4, 2, 4), (*ctx, "tp"))
    return jax.shard_map(
        on_device,
        mesh=fine,
        in_specs=(
            P((*ctx, "tp"), None),
            P((*ctx, "tp"), None),
            P((*ctx, "tp"), None),
            P(None, "tp"),
            P("tp"),
        ),
        out_specs=P(ctx, "tp"),
        check_vma=False,
    )
```

```python
import math

import jax
import jax.numpy as jnp
import numpy as np
from jax import lax
from jax.experimental import pallas as pl
from jax.experimental.pallas import tpu as pltpu
from jax.sharding import Mesh, PartitionSpec as P

HEAD_DIM = 128
LOG2E = 1.4426950408889634
SCALE = HEAD_DIM ** -0.5
AXES = ("zl", "y", "x", "c", "tp")
HEAD_AXES = ("zl", "c", "tp")
QUERY_AXES = ("x",)
KEY_AXES = ("y",)
STATS = 2
STAT_LANES = 8
STAT_ROWS = 16
GROUP_STEP = 1
EARLY_HEADS = 6
KERNEL_VMEM = 16 * 1024 * 1024
MIX_VMEM = 50 * 1024 * 1024
IN_VMEM = pl.BlockSpec(memory_space=pltpu.VMEM)


def pack_stats(columns):
    tokens = columns[0][0].shape[0]
    lane = lax.broadcasted_iota(jnp.int32, (tokens, HEAD_DIM), 1)
    stats = jnp.zeros((tokens, HEAD_DIM), jnp.float32)
    for group, values in enumerate(columns):
        for place, value in enumerate(values):
            stats = jnp.where(lane == group * STAT_LANES + place, value, stats)
    high = stats.astype(jnp.bfloat16).astype(jnp.float32)
    rest = stats - high
    middle = rest.astype(jnp.bfloat16).astype(jnp.float32)
    low = rest - middle
    pieces = high + pltpu.roll(middle, STATS, 1) + pltpu.roll(low, 2 * STATS, 1)
    filler = jnp.zeros((2 * HEAD_DIM - tokens, HEAD_DIM), jnp.float32)
    rows = jnp.concatenate([pieces, filler], axis=0).T
    packed = []
    for group in range(len(columns)):
        own = rows[group * STAT_LANES : (group + 1) * STAT_LANES]
        both = jnp.concatenate([own[:, :HEAD_DIM], own[:, HEAD_DIM:]], axis=0)
        packed.append(both.astype(jnp.bfloat16))
    return packed


def unpack_stats(packed, tokens):
    groups = packed.shape[0]
    rows = packed.astype(jnp.float32)
    filler = jnp.zeros((HEAD_DIM - groups * STAT_LANES, HEAD_DIM), jnp.float32)
    halves = [
        jnp.concatenate(
            [rows[group, half : half + STAT_LANES] for group in range(groups)] + [filler], axis=0
        )
        for half in (0, STAT_LANES)
    ]
    pieces = jnp.concatenate([half.T for half in halves], axis=0)[:tokens]
    return (
        pieces
        + pltpu.roll(pieces, HEAD_DIM - STATS, 1)
        + pltpu.roll(pieces, HEAD_DIM - 2 * STATS, 1)
    )


def split_kernel(local_ref, query_ref, key_value_ref):
    slots = local_ref.shape[0]
    rows = local_ref.shape[1] // 3
    query_ref[...] = local_ref[:, pl.ds(0, rows)].reshape(slots * rows, HEAD_DIM)
    for place in range(2):
        block = local_ref[:, pl.ds((place + 1) * rows, rows)].reshape(slots * rows, HEAD_DIM)
        for copy in range(key_value_ref.shape[0]):
            key_value_ref[copy, place] = block


def attend_kernel(q_ref, key_value_ref, out_ref):
    groups, tokens, width = q_ref.shape
    count = key_value_ref.shape[0] * tokens
    key = key_value_ref[:, 0].reshape(count, width)
    value = key_value_ref[:, 1].reshape(count, width)
    columns = []
    for group in range(0, groups, GROUP_STEP):
        query = q_ref[pl.ds(group, GROUP_STEP)].reshape(GROUP_STEP * tokens, width)
        score = lax.dot_general(
            query, key, (((1,), (1,)), ((), ())), preferred_element_type=jnp.float32
        )
        highest = jnp.max(score, axis=1, keepdims=True)
        expd = jnp.exp2((score - highest) * (SCALE * LOG2E))
        total = jnp.sum(expd, axis=1, keepdims=True)
        summed = jnp.dot(expd.astype(jnp.bfloat16), value, preferred_element_type=jnp.float32)
        for step in range(GROUP_STEP):
            rows = slice(step * tokens, (step + 1) * tokens)
            out_ref[group + step, pl.ds(0, tokens)] = summed[rows].astype(jnp.bfloat16)
            columns.append((highest[rows], total[rows]))
    for group, packed in enumerate(pack_stats(columns)):
        out_ref[group, pl.ds(tokens, STAT_ROWS)] = packed


def combine_kernel(part_ref, out_ref):
    groups = part_ref.shape[0]
    tokens = part_ref.shape[1] - STAT_ROWS
    copies, rows, _ = out_ref.shape
    stats = unpack_stats(part_ref[:, pl.ds(tokens, STAT_ROWS)], tokens)
    lane = lax.broadcasted_iota(jnp.int32, stats.shape, 1)
    is_maximum = (lane % STAT_LANES == 0) & (lane < groups * STAT_LANES)
    highest = jnp.max(jnp.where(is_maximum, stats, -jnp.inf), axis=1, keepdims=True)
    weight = jnp.where(is_maximum, jnp.exp2((stats - highest) * (SCALE * LOG2E)), 0.0)
    sums = jnp.where(is_maximum, pltpu.roll(stats, HEAD_DIM - 1, 1), 0.0)
    total = jnp.sum(weight * sums, axis=1, keepdims=True)
    summed = jnp.zeros(stats.shape, jnp.float32)
    for group in range(groups):
        at = group * STAT_LANES
        part = part_ref[group, pl.ds(0, tokens)].astype(jnp.float32)
        summed += part * weight[:, at : at + 1]
    attended = (summed / total).astype(jnp.bfloat16)
    repeats = copies * rows // tokens
    for block in range(tokens // rows):
        for repeat in range(repeats):
            out_ref[block * repeats + repeat] = attended[block * rows : (block + 1) * rows]


def load_rows(weight_ref, held_ref, semaphores, first):
    rows = held_ref.shape[0] // semaphores.shape[0]
    copies = []
    for piece in range(semaphores.shape[0]):
        copy = pltpu.make_async_copy(
            weight_ref.at[pl.ds(first + piece * rows, rows)],
            held_ref.at[pl.ds(piece * rows, rows)],
            semaphores.at[piece],
        )
        copy.start()
        copies.append(copy)
    return copies


def fetch_kernel(weight_ref, gate_ref, held_ref, row_ref, semaphores):
    copies = load_rows(weight_ref, held_ref, semaphores, 0)
    row_ref[...] = gate_ref[...][None, :]
    for copy in copies:
        copy.wait()


def mix_kernel(attended_ref, row_ref, first_ref, weight_ref, out_ref, held_ref, semaphores):
    early = first_ref.shape[0] // HEAD_DIM
    copies = load_rows(weight_ref, held_ref, semaphores, first_ref.shape[0])
    span = held_ref.shape[0] // HEAD_DIM // len(copies)

    def product_of(first, count, rows):
        block = jnp.concatenate(
            [attended_ref[head] for head in range(first, first + count)], axis=1
        )
        return jnp.dot(block, rows, preferred_element_type=jnp.float32)

    product = product_of(0, early, first_ref[...])
    for piece, copy in enumerate(copies):
        copy.wait()
        rows = held_ref[pl.ds(piece * span * HEAD_DIM, span * HEAD_DIM)]
        product += product_of(early + piece * span, span, rows)
    out_ref[...] = (product * row_ref[...]).astype(jnp.bfloat16)


def listed_groups(axes):
    sizes = [lax.axis_size(axis) for axis in AXES]
    places = np.arange(math.prod(sizes)).reshape(sizes)
    inner = [AXES.index(axis) for axis in axes]
    outer = [place for place in range(len(AXES)) if place not in inner]
    members = math.prod(sizes[place] for place in inner)
    return places.transpose(outer + inner).reshape(-1, members).tolist()


def exchange(blocks, axes):
    return lax.all_to_all(
        blocks, AXES, split_axis=0, concat_axis=0, axis_index_groups=listed_groups(axes), tiled=True
    )


def on_device(queries, keys, vals, out_weight, gate):
    slots = lax.axis_size(HEAD_AXES)
    rows, width = queries.shape
    heads = width // HEAD_DIM
    tokens = slots * rows
    own_tokens = lax.axis_size("tp") * rows
    stacked = jnp.stack([queries, keys, vals], axis=0).reshape(3, rows, heads, HEAD_DIM)
    stacked = stacked.transpose(2, 0, 1, 3).reshape(heads, 3 * rows, HEAD_DIM)
    stacked = jnp.pad(stacked, ((0, slots - heads), (0, 0), (0, 0)))
    own_query, key_value_copies = pl.pallas_call(
        split_kernel,
        out_shape=[
            jax.ShapeDtypeStruct((tokens, HEAD_DIM), jnp.bfloat16),
            jax.ShapeDtypeStruct((lax.axis_size(KEY_AXES), 2, tokens, HEAD_DIM), jnp.bfloat16),
        ],
        in_specs=[IN_VMEM],
        out_specs=[IN_VMEM] * 2,
        compiler_params=pltpu.CompilerParams(vmem_limit_bytes=KERNEL_VMEM),
        name="split",
    )(exchange(stacked, HEAD_AXES))
    channels = out_weight.shape[1]
    key_value_copies, weight = lax.optimization_barrier((key_value_copies, out_weight))
    in_hbm = pl.BlockSpec(memory_space=pltpu.HBM)
    first, row = pl.pallas_call(
        fetch_kernel,
        out_shape=[
            jax.ShapeDtypeStruct((EARLY_HEADS * HEAD_DIM, channels), weight.dtype),
            jax.ShapeDtypeStruct((1, channels), gate.dtype),
        ],
        in_specs=[in_hbm, IN_VMEM],
        out_specs=[IN_VMEM] * 2,
        scratch_shapes=[pltpu.SemaphoreType.DMA((EARLY_HEADS // 2,))],
        compiler_params=pltpu.CompilerParams(vmem_limit_bytes=MIX_VMEM),
        cost_estimate=pl.CostEstimate(
            flops=0, bytes_accessed=4 * EARLY_HEADS * HEAD_DIM * channels, transcendentals=0
        ),
        name="fetch",
    )(weight, gate)
    key_value = exchange(key_value_copies, KEY_AXES)
    group = lax.all_gather(own_query, QUERY_AXES, axis=0, tiled=False)
    key_value, group, first, row = lax.optimization_barrier((key_value, group, first, row))
    partial = pl.pallas_call(
        attend_kernel,
        out_shape=jax.ShapeDtypeStruct(
            (group.shape[0], tokens + STAT_ROWS, HEAD_DIM), jnp.bfloat16
        ),
        in_specs=[IN_VMEM] * 2,
        out_specs=IN_VMEM,
        compiler_params=pltpu.CompilerParams(vmem_limit_bytes=KERNEL_VMEM),
        name="attend",
    )(group, key_value)
    partial = exchange(partial, QUERY_AXES)
    attended = pl.pallas_call(
        combine_kernel,
        out_shape=jax.ShapeDtypeStruct((slots, own_tokens, HEAD_DIM), jnp.bfloat16),
        in_specs=[IN_VMEM],
        out_specs=IN_VMEM,
        compiler_params=pltpu.CompilerParams(vmem_limit_bytes=KERNEL_VMEM),
        name="combine",
    )(partial)
    attended = exchange(attended, HEAD_AXES)
    late = heads - EARLY_HEADS
    return pl.pallas_call(
        mix_kernel,
        out_shape=jax.ShapeDtypeStruct((own_tokens, channels), jnp.bfloat16),
        in_specs=[IN_VMEM, IN_VMEM, IN_VMEM, in_hbm],
        out_specs=IN_VMEM,
        scratch_shapes=[
            pltpu.VMEM((late * HEAD_DIM, channels), out_weight.dtype),
            pltpu.SemaphoreType.DMA((late // 2,)),
        ],
        compiler_params=pltpu.CompilerParams(vmem_limit_bytes=MIX_VMEM),
        name="mix",
    )(attended, row, first, weight)


def solution(mesh):
    ctx = ("zl", "y", "x", "c")
    fine = Mesh(mesh.devices.reshape(3, 8, 4, 2, 4), (*ctx, "tp"))
    return jax.shard_map(
        on_device,
        mesh=fine,
        in_specs=(
            P((*ctx, "tp"), None),
            P((*ctx, "tp"), None),
            P((*ctx, "tp"), None),
            P(None, "tp"),
            P("tp"),
        ),
        out_specs=P(ctx, "tp"),
        check_vma=False,
    )
```

```python
import functools

import jax
import jax.numpy as jnp
from jax import lax
from jax.experimental import pallas as pl
from jax.experimental.pallas import tpu as pltpu
from jax.sharding import Mesh, PartitionSpec as P

HEAD_DIM = 128
LOG2E = 1.4426950408889634
SCALE = HEAD_DIM ** -0.5
HEAD_AXES = ("zl", "c", "tp")
QUERY_AXES = ("x",)
KEY_AXES = ("y",)
STATS = 2
STAT_LANES = 8
STAT_ROWS = 16
GROUP_STEP = 2
KEY_BLOCKS = 4
EARLY_HEADS = 6
KERNEL_VMEM = 16 * 1024 * 1024
MIX_VMEM = 50 * 1024 * 1024
IN_VMEM = pl.BlockSpec(memory_space=pltpu.VMEM)


def pack_stats(columns):
    tokens = columns[0][0].shape[0]
    lane = lax.broadcasted_iota(jnp.int32, (tokens, HEAD_DIM), 1)
    stats = jnp.zeros((tokens, HEAD_DIM), jnp.float32)
    for group, values in enumerate(columns):
        for place, value in enumerate(values):
            stats = jnp.where(lane == group * STAT_LANES + place, value, stats)
    high = stats.astype(jnp.bfloat16).astype(jnp.float32)
    rest = stats - high
    middle = rest.astype(jnp.bfloat16).astype(jnp.float32)
    low = rest - middle
    pieces = high + pltpu.roll(middle, STATS, 1) + pltpu.roll(low, 2 * STATS, 1)
    filler = jnp.zeros((2 * HEAD_DIM - tokens, HEAD_DIM), jnp.float32)
    rows = jnp.concatenate([pieces, filler], axis=0).T
    packed = []
    for group in range(len(columns)):
        own = rows[group * STAT_LANES : (group + 1) * STAT_LANES]
        both = jnp.concatenate([own[:, :HEAD_DIM], own[:, HEAD_DIM:]], axis=0)
        packed.append(both.astype(jnp.bfloat16))
    return packed


def unpack_stats(packed, tokens):
    groups = packed.shape[0]
    rows = packed.astype(jnp.float32)
    filler = jnp.zeros((HEAD_DIM - groups * STAT_LANES, HEAD_DIM), jnp.float32)
    halves = [
        jnp.concatenate(
            [rows[group, half : half + STAT_LANES] for group in range(groups)] + [filler], axis=0
        )
        for half in (0, STAT_LANES)
    ]
    pieces = jnp.concatenate([half.T for half in halves], axis=0)[:tokens]
    return (
        pieces
        + pltpu.roll(pieces, HEAD_DIM - STATS, 1)
        + pltpu.roll(pieces, HEAD_DIM - 2 * STATS, 1)
    )


def split_kernel(local_ref, query_ref, key_value_ref, block_ref, semaphores):
    slots = local_ref.shape[0]
    rows = local_ref.shape[1] // 3
    for place in range(2):
        block = local_ref[:, pl.ds((place + 1) * rows, rows)]
        block_ref[place] = block.reshape(slots * rows, HEAD_DIM)
    copies = []
    for copy in range(key_value_ref.shape[0]):
        copies.append(
            pltpu.make_async_copy(block_ref, key_value_ref.at[copy], semaphores.at[copy])
        )
        copies[copy].start()
    query_ref[...] = local_ref[:, pl.ds(0, rows)].reshape(slots * rows, HEAD_DIM)
    for copy in copies:
        copy.wait()


def attend_kernel(q_ref, key_value_ref, out_ref):
    groups, tokens, width = q_ref.shape
    blocks = key_value_ref.shape[0] // KEY_BLOCKS
    count = blocks * tokens
    columns = []
    for group in range(0, groups, GROUP_STEP):
        query = q_ref[pl.ds(group, GROUP_STEP)].reshape(GROUP_STEP * tokens, width)
        scores = []
        for block in range(KEY_BLOCKS):
            key = key_value_ref[pl.ds(block * blocks, blocks), 0].reshape(count, width)
            scores.append(
                lax.dot_general(
                    query, key, (((1,), (1,)), ((), ())), preferred_element_type=jnp.float32
                )
            )
        highest = functools.reduce(
            jnp.maximum, [jnp.max(score, axis=1, keepdims=True) for score in scores]
        )
        total, summed = 0.0, 0.0
        for block, score in enumerate(scores):
            value = key_value_ref[pl.ds(block * blocks, blocks), 1].reshape(count, width)
            expd = jnp.exp2((score - highest) * (SCALE * LOG2E))
            total += jnp.sum(expd, axis=1, keepdims=True)
            summed += jnp.dot(expd.astype(jnp.bfloat16), value, preferred_element_type=jnp.float32)
        for step in range(GROUP_STEP):
            rows = slice(step * tokens, (step + 1) * tokens)
            out_ref[group + step, pl.ds(0, tokens)] = summed[rows].astype(jnp.bfloat16)
            columns.append((highest[rows], total[rows]))
    for group, packed in enumerate(pack_stats(columns)):
        out_ref[group, pl.ds(tokens, STAT_ROWS)] = packed


def combine_kernel(part_ref, out_ref):
    groups = part_ref.shape[0]
    tokens = part_ref.shape[1] - STAT_ROWS
    copies, rows, _ = out_ref.shape
    stats = unpack_stats(part_ref[:, pl.ds(tokens, STAT_ROWS)], tokens)
    lane = lax.broadcasted_iota(jnp.int32, stats.shape, 1)
    is_maximum = (lane % STAT_LANES == 0) & (lane < groups * STAT_LANES)
    highest = jnp.max(jnp.where(is_maximum, stats, -jnp.inf), axis=1, keepdims=True)
    weight = jnp.where(is_maximum, jnp.exp2((stats - highest) * (SCALE * LOG2E)), 0.0)
    sums = jnp.where(is_maximum, pltpu.roll(stats, HEAD_DIM - 1, 1), 0.0)
    total = jnp.sum(weight * sums, axis=1, keepdims=True)
    summed = jnp.zeros(stats.shape, jnp.float32)
    for group in range(groups):
        at = group * STAT_LANES
        part = part_ref[group, pl.ds(0, tokens)].astype(jnp.float32)
        summed += part * weight[:, at : at + 1]
    attended = (summed / total).astype(jnp.bfloat16)
    repeats = copies * rows // tokens
    for block in range(tokens // rows):
        for repeat in range(repeats):
            out_ref[block * repeats + repeat] = attended[block * rows : (block + 1) * rows]


def load_rows(weight_ref, held_ref, semaphores, first):
    rows = held_ref.shape[0] // semaphores.shape[0]
    copies = []
    for piece in range(semaphores.shape[0]):
        copy = pltpu.make_async_copy(
            weight_ref.at[pl.ds(first + piece * rows, rows)],
            held_ref.at[pl.ds(piece * rows, rows)],
            semaphores.at[piece],
        )
        copy.start()
        copies.append(copy)
    return copies


def fetch_kernel(weight_ref, gate_ref, held_ref, row_ref, semaphores):
    copies = load_rows(weight_ref, held_ref, semaphores, 0)
    row_ref[...] = gate_ref[...][None, :]
    for copy in copies:
        copy.wait()


def mix_kernel(attended_ref, row_ref, first_ref, weight_ref, out_ref, held_ref, semaphores):
    early = first_ref.shape[0] // HEAD_DIM
    copies = load_rows(weight_ref, held_ref, semaphores, first_ref.shape[0])
    span = held_ref.shape[0] // HEAD_DIM // len(copies)

    def product_of(first, count, rows):
        block = jnp.concatenate(
            [attended_ref[head] for head in range(first, first + count)], axis=1
        )
        return jnp.dot(block, rows, preferred_element_type=jnp.float32)

    product = product_of(0, early, first_ref[...])
    for piece, copy in enumerate(copies):
        copy.wait()
        rows = held_ref[pl.ds(piece * span * HEAD_DIM, span * HEAD_DIM)]
        product += product_of(early + piece * span, span, rows)
    out_ref[...] = (product * row_ref[...]).astype(jnp.bfloat16)


def exchange(blocks, axes):
    return lax.all_to_all(blocks, axes, split_axis=0, concat_axis=0, tiled=True)


def on_device(queries, keys, vals, out_weight, gate):
    slots = lax.axis_size(HEAD_AXES)
    rows, width = queries.shape
    heads = width // HEAD_DIM
    tokens = slots * rows
    own_tokens = lax.axis_size("tp") * rows
    stacked = jnp.stack([queries, keys, vals], axis=0).reshape(3, rows, heads, HEAD_DIM)
    stacked = stacked.transpose(2, 0, 1, 3).reshape(heads, 3 * rows, HEAD_DIM)
    stacked = jnp.pad(stacked, ((0, slots - heads), (0, 0), (0, 0)))
    own_query, key_value_copies = pl.pallas_call(
        split_kernel,
        out_shape=[
            jax.ShapeDtypeStruct((tokens, HEAD_DIM), jnp.bfloat16),
            jax.ShapeDtypeStruct((lax.axis_size(KEY_AXES), 2, tokens, HEAD_DIM), jnp.bfloat16),
        ],
        in_specs=[IN_VMEM],
        out_specs=[IN_VMEM, pl.BlockSpec(memory_space=pltpu.HBM)],
        scratch_shapes=[
            pltpu.VMEM((2, tokens, HEAD_DIM), jnp.bfloat16),
            pltpu.SemaphoreType.DMA((lax.axis_size(KEY_AXES),)),
        ],
        compiler_params=pltpu.CompilerParams(vmem_limit_bytes=KERNEL_VMEM),
        name="split",
    )(exchange(stacked, HEAD_AXES))
    channels = out_weight.shape[1]
    key_value_copies, weight = lax.optimization_barrier((key_value_copies, out_weight))
    in_hbm = pl.BlockSpec(memory_space=pltpu.HBM)
    first, row = pl.pallas_call(
        fetch_kernel,
        out_shape=[
            jax.ShapeDtypeStruct((EARLY_HEADS * HEAD_DIM, channels), weight.dtype),
            jax.ShapeDtypeStruct((1, channels), gate.dtype),
        ],
        in_specs=[in_hbm, IN_VMEM],
        out_specs=[IN_VMEM] * 2,
        scratch_shapes=[pltpu.SemaphoreType.DMA((EARLY_HEADS // 2,))],
        compiler_params=pltpu.CompilerParams(vmem_limit_bytes=MIX_VMEM),
        cost_estimate=pl.CostEstimate(
            flops=0, bytes_accessed=4 * EARLY_HEADS * HEAD_DIM * channels, transcendentals=0
        ),
        name="fetch",
    )(weight, gate)
    key_value = exchange(key_value_copies, KEY_AXES)
    group = lax.all_gather(own_query, QUERY_AXES, axis=0, tiled=False)
    key_value, group, first, row = lax.optimization_barrier((key_value, group, first, row))
    partial = pl.pallas_call(
        attend_kernel,
        out_shape=jax.ShapeDtypeStruct(
            (group.shape[0], tokens + STAT_ROWS, HEAD_DIM), jnp.bfloat16
        ),
        in_specs=[IN_VMEM] * 2,
        out_specs=IN_VMEM,
        compiler_params=pltpu.CompilerParams(vmem_limit_bytes=KERNEL_VMEM),
        name="attend",
    )(group, key_value)
    partial = exchange(partial, QUERY_AXES)
    attended = pl.pallas_call(
        combine_kernel,
        out_shape=jax.ShapeDtypeStruct((slots, own_tokens, HEAD_DIM), jnp.bfloat16),
        in_specs=[IN_VMEM],
        out_specs=IN_VMEM,
        compiler_params=pltpu.CompilerParams(vmem_limit_bytes=KERNEL_VMEM),
        name="combine",
    )(partial)
    attended = exchange(attended, HEAD_AXES)
    late = heads - EARLY_HEADS
    return pl.pallas_call(
        mix_kernel,
        out_shape=jax.ShapeDtypeStruct((own_tokens, channels), jnp.bfloat16),
        in_specs=[IN_VMEM, IN_VMEM, IN_VMEM, in_hbm],
        out_specs=IN_VMEM,
        scratch_shapes=[
            pltpu.VMEM((late * HEAD_DIM, channels), out_weight.dtype),
            pltpu.SemaphoreType.DMA((late // 2,)),
        ],
        compiler_params=pltpu.CompilerParams(vmem_limit_bytes=MIX_VMEM),
        name="mix",
    )(attended, row, first, weight)


def solution(mesh):
    ctx = ("zl", "y", "x", "c")
    fine = Mesh(mesh.devices.reshape(3, 8, 4, 2, 4), (*ctx, "tp"))
    return jax.shard_map(
        on_device,
        mesh=fine,
        in_specs=(
            P((*ctx, "tp"), None),
            P((*ctx, "tp"), None),
            P((*ctx, "tp"), None),
            P(None, "tp"),
            P("tp"),
        ),
        out_specs=P(ctx, "tp"),
        check_vma=False,
    )
```

```python
import functools

import jax
import jax.numpy as jnp
from jax import lax
from jax.experimental import pallas as pl
from jax.experimental.pallas import tpu as pltpu
from jax.sharding import Mesh, PartitionSpec as P

HEAD_DIM = 128
LOG2E = 1.4426950408889634
SCALE = HEAD_DIM ** -0.5
HEAD_AXES = ("c", "zl", "tp")
QUERY_AXES = ("x",)
KEY_AXES = ("y",)
STATS = 2
STAT_LANES = 8
STAT_ROWS = 16
GROUP_STEP = 2
KEY_BLOCKS = 4
EARLY_HEADS = 6
KERNEL_VMEM = 16 * 1024 * 1024
MIX_VMEM = 50 * 1024 * 1024
IN_VMEM = pl.BlockSpec(memory_space=pltpu.VMEM)


def pack_stats(columns):
    tokens = columns[0][0].shape[0]
    lane = lax.broadcasted_iota(jnp.int32, (tokens, HEAD_DIM), 1)
    stats = jnp.zeros((tokens, HEAD_DIM), jnp.float32)
    for group, values in enumerate(columns):
        for place, value in enumerate(values):
            stats = jnp.where(lane == group * STAT_LANES + place, value, stats)
    high = stats.astype(jnp.bfloat16).astype(jnp.float32)
    rest = stats - high
    middle = rest.astype(jnp.bfloat16).astype(jnp.float32)
    low = rest - middle
    pieces = high + pltpu.roll(middle, STATS, 1) + pltpu.roll(low, 2 * STATS, 1)
    filler = jnp.zeros((2 * HEAD_DIM - tokens, HEAD_DIM), jnp.float32)
    rows = jnp.concatenate([pieces, filler], axis=0).T
    packed = []
    for group in range(len(columns)):
        own = rows[group * STAT_LANES : (group + 1) * STAT_LANES]
        both = jnp.concatenate([own[:, :HEAD_DIM], own[:, HEAD_DIM:]], axis=0)
        packed.append(both.astype(jnp.bfloat16))
    return packed


def unpack_stats(packed, tokens):
    groups = packed.shape[0]
    rows = packed.astype(jnp.float32)
    filler = jnp.zeros((HEAD_DIM - groups * STAT_LANES, HEAD_DIM), jnp.float32)
    halves = [
        jnp.concatenate(
            [rows[group, half : half + STAT_LANES] for group in range(groups)] + [filler], axis=0
        )
        for half in (0, STAT_LANES)
    ]
    pieces = jnp.concatenate([half.T for half in halves], axis=0)[:tokens]
    return (
        pieces
        + pltpu.roll(pieces, HEAD_DIM - STATS, 1)
        + pltpu.roll(pieces, HEAD_DIM - 2 * STATS, 1)
    )


def split_kernel(local_ref, query_ref, key_value_ref, block_ref, semaphores):
    slots = local_ref.shape[0]
    rows = local_ref.shape[1] // 3
    for place in range(2):
        block = local_ref[:, pl.ds((place + 1) * rows, rows)]
        block_ref[place] = block.reshape(slots * rows, HEAD_DIM)
    copies = []
    for copy in range(key_value_ref.shape[0]):
        copies.append(
            pltpu.make_async_copy(block_ref, key_value_ref.at[copy], semaphores.at[copy])
        )
        copies[copy].start()
    query_ref[...] = local_ref[:, pl.ds(0, rows)].reshape(slots * rows, HEAD_DIM)
    for copy in copies:
        copy.wait()


def attend_kernel(q_ref, key_value_ref, out_ref):
    groups, tokens, width = q_ref.shape
    blocks = key_value_ref.shape[0] // KEY_BLOCKS
    count = blocks * tokens
    columns = []
    for group in range(0, groups, GROUP_STEP):
        query = q_ref[pl.ds(group, GROUP_STEP)].reshape(GROUP_STEP * tokens, width)
        scores = []
        for block in range(KEY_BLOCKS):
            key = key_value_ref[pl.ds(block * blocks, blocks), 0].reshape(count, width)
            scores.append(
                lax.dot_general(
                    query, key, (((1,), (1,)), ((), ())), preferred_element_type=jnp.float32
                )
            )
        highest = functools.reduce(
            jnp.maximum, [jnp.max(score, axis=1, keepdims=True) for score in scores]
        )
        total, summed = 0.0, 0.0
        for block, score in enumerate(scores):
            value = key_value_ref[pl.ds(block * blocks, blocks), 1].reshape(count, width)
            expd = jnp.exp2((score - highest) * (SCALE * LOG2E))
            total += jnp.sum(expd, axis=1, keepdims=True)
            summed += jnp.dot(expd.astype(jnp.bfloat16), value, preferred_element_type=jnp.float32)
        for step in range(GROUP_STEP):
            rows = slice(step * tokens, (step + 1) * tokens)
            out_ref[group + step, pl.ds(0, tokens)] = summed[rows].astype(jnp.bfloat16)
            columns.append((highest[rows], total[rows]))
    for group, packed in enumerate(pack_stats(columns)):
        out_ref[group, pl.ds(tokens, STAT_ROWS)] = packed


def combine_kernel(part_ref, out_ref):
    groups = part_ref.shape[0]
    tokens = part_ref.shape[1] - STAT_ROWS
    copies, rows, _ = out_ref.shape
    stats = unpack_stats(part_ref[:, pl.ds(tokens, STAT_ROWS)], tokens)
    lane = lax.broadcasted_iota(jnp.int32, stats.shape, 1)
    is_maximum = (lane % STAT_LANES == 0) & (lane < groups * STAT_LANES)
    highest = jnp.max(jnp.where(is_maximum, stats, -jnp.inf), axis=1, keepdims=True)
    weight = jnp.where(is_maximum, jnp.exp2((stats - highest) * (SCALE * LOG2E)), 0.0)
    sums = jnp.where(is_maximum, pltpu.roll(stats, HEAD_DIM - 1, 1), 0.0)
    total = jnp.sum(weight * sums, axis=1, keepdims=True)
    summed = jnp.zeros(stats.shape, jnp.float32)
    for group in range(groups):
        at = group * STAT_LANES
        part = part_ref[group, pl.ds(0, tokens)].astype(jnp.float32)
        summed += part * weight[:, at : at + 1]
    attended = (summed / total).astype(jnp.bfloat16)
    repeats = copies * rows // tokens
    for block in range(tokens // rows):
        for repeat in range(repeats):
            out_ref[block * repeats + repeat] = attended[block * rows : (block + 1) * rows]


def load_rows(weight_ref, held_ref, semaphores, first):
    rows = held_ref.shape[0] // semaphores.shape[0]
    copies = []
    for piece in range(semaphores.shape[0]):
        copy = pltpu.make_async_copy(
            weight_ref.at[pl.ds(first + piece * rows, rows)],
            held_ref.at[pl.ds(piece * rows, rows)],
            semaphores.at[piece],
        )
        copy.start()
        copies.append(copy)
    return copies


def fetch_kernel(weight_ref, gate_ref, held_ref, row_ref, semaphores):
    copies = load_rows(weight_ref, held_ref, semaphores, 0)
    row_ref[...] = gate_ref[...][None, :]
    for copy in copies:
        copy.wait()


def mix_kernel(attended_ref, row_ref, first_ref, weight_ref, out_ref, held_ref, semaphores):
    early = first_ref.shape[0] // HEAD_DIM
    copies = load_rows(weight_ref, held_ref, semaphores, first_ref.shape[0])
    span = held_ref.shape[0] // HEAD_DIM // len(copies)

    def product_of(first, count, rows):
        block = jnp.concatenate(
            [attended_ref[head] for head in range(first, first + count)], axis=1
        )
        return jnp.dot(block, rows, preferred_element_type=jnp.float32)

    product = product_of(0, early, first_ref[...])
    for piece, copy in enumerate(copies):
        copy.wait()
        rows = held_ref[pl.ds(piece * span * HEAD_DIM, span * HEAD_DIM)]
        product += product_of(early + piece * span, span, rows)
    out_ref[...] = (product * row_ref[...]).astype(jnp.bfloat16)


def exchange(blocks, axes):
    return lax.all_to_all(blocks, axes, split_axis=0, concat_axis=0, tiled=True)


def on_device(queries, keys, vals, out_weight, gate):
    slots = lax.axis_size(HEAD_AXES)
    rows, width = queries.shape
    heads = width // HEAD_DIM
    tokens = slots * rows
    own_tokens = lax.axis_size("tp") * rows
    stacked = jnp.stack([queries, keys, vals], axis=0).reshape(3, rows, heads, HEAD_DIM)
    stacked = stacked.transpose(2, 0, 1, 3).reshape(heads, 3 * rows, HEAD_DIM)
    stacked = jnp.pad(stacked, ((0, slots - heads), (0, 0), (0, 0)))
    own_query, key_value_copies = pl.pallas_call(
        split_kernel,
        out_shape=[
            jax.ShapeDtypeStruct((tokens, HEAD_DIM), jnp.bfloat16),
            jax.ShapeDtypeStruct((lax.axis_size(KEY_AXES), 2, tokens, HEAD_DIM), jnp.bfloat16),
        ],
        in_specs=[IN_VMEM],
        out_specs=[IN_VMEM, pl.BlockSpec(memory_space=pltpu.HBM)],
        scratch_shapes=[
            pltpu.VMEM((2, tokens, HEAD_DIM), jnp.bfloat16),
            pltpu.SemaphoreType.DMA((lax.axis_size(KEY_AXES),)),
        ],
        compiler_params=pltpu.CompilerParams(vmem_limit_bytes=KERNEL_VMEM),
        name="split",
    )(exchange(stacked, HEAD_AXES))
    channels = out_weight.shape[1]
    key_value_copies, weight = lax.optimization_barrier((key_value_copies, out_weight))
    in_hbm = pl.BlockSpec(memory_space=pltpu.HBM)
    first, row = pl.pallas_call(
        fetch_kernel,
        out_shape=[
            jax.ShapeDtypeStruct((EARLY_HEADS * HEAD_DIM, channels), weight.dtype),
            jax.ShapeDtypeStruct((1, channels), gate.dtype),
        ],
        in_specs=[in_hbm, IN_VMEM],
        out_specs=[IN_VMEM] * 2,
        scratch_shapes=[pltpu.SemaphoreType.DMA((EARLY_HEADS // 2,))],
        compiler_params=pltpu.CompilerParams(vmem_limit_bytes=MIX_VMEM),
        cost_estimate=pl.CostEstimate(
            flops=0, bytes_accessed=4 * EARLY_HEADS * HEAD_DIM * channels, transcendentals=0
        ),
        name="fetch",
    )(weight, gate)
    key_value = exchange(key_value_copies, KEY_AXES)
    group = lax.all_gather(own_query, QUERY_AXES, axis=0, tiled=False)
    key_value, group, first, row = lax.optimization_barrier((key_value, group, first, row))
    partial = pl.pallas_call(
        attend_kernel,
        out_shape=jax.ShapeDtypeStruct(
            (group.shape[0], tokens + STAT_ROWS, HEAD_DIM), jnp.bfloat16
        ),
        in_specs=[IN_VMEM] * 2,
        out_specs=IN_VMEM,
        compiler_params=pltpu.CompilerParams(vmem_limit_bytes=KERNEL_VMEM),
        name="attend",
    )(group, key_value)
    partial = exchange(partial, QUERY_AXES)
    attended = pl.pallas_call(
        combine_kernel,
        out_shape=jax.ShapeDtypeStruct((slots, own_tokens, HEAD_DIM), jnp.bfloat16),
        in_specs=[IN_VMEM],
        out_specs=IN_VMEM,
        compiler_params=pltpu.CompilerParams(vmem_limit_bytes=KERNEL_VMEM),
        name="combine",
    )(partial)
    attended = exchange(attended, HEAD_AXES)
    late = heads - EARLY_HEADS
    return pl.pallas_call(
        mix_kernel,
        out_shape=jax.ShapeDtypeStruct((own_tokens, channels), jnp.bfloat16),
        in_specs=[IN_VMEM, IN_VMEM, IN_VMEM, in_hbm],
        out_specs=IN_VMEM,
        scratch_shapes=[
            pltpu.VMEM((late * HEAD_DIM, channels), out_weight.dtype),
            pltpu.SemaphoreType.DMA((late // 2,)),
        ],
        compiler_params=pltpu.CompilerParams(vmem_limit_bytes=MIX_VMEM),
        name="mix",
    )(attended, row, first, weight)


def solution(mesh):
    ctx = ("zl", "y", "x", "c")
    fine = Mesh(mesh.devices.reshape(3, 8, 4, 2, 4), (*ctx, "tp"))
    return jax.shard_map(
        on_device,
        mesh=fine,
        in_specs=(
            P((*ctx, "tp"), None),
            P((*ctx, "tp"), None),
            P((*ctx, "tp"), None),
            P(None, "tp"),
            P("tp"),
        ),
        out_specs=P(ctx, "tp"),
        check_vma=False,
    )
```

```python
import functools

import jax
import jax.numpy as jnp
from jax import lax
from jax.experimental import pallas as pl
from jax.experimental.pallas import tpu as pltpu
from jax.sharding import Mesh, PartitionSpec as P

HEAD_DIM = 128
LOG2E = 1.4426950408889634
SCALE = HEAD_DIM ** -0.5
HEAD_AXES = ("zl", "c", "tp")
QUERY_AXES = ("x",)
KEY_AXES = ("y",)
STATS = 2
STAT_LANES = 8
STAT_ROWS = 16
GROUP_STEP = 2
KEY_BLOCKS = 4
EARLY_HEADS = 7
KERNEL_VMEM = 16 * 1024 * 1024
MIX_VMEM = 50 * 1024 * 1024
IN_VMEM = pl.BlockSpec(memory_space=pltpu.VMEM)


def pack_stats(columns):
    tokens = columns[0][0].shape[0]
    lane = lax.broadcasted_iota(jnp.int32, (tokens, HEAD_DIM), 1)
    stats = jnp.zeros((tokens, HEAD_DIM), jnp.float32)
    for group, values in enumerate(columns):
        for place, value in enumerate(values):
            stats = jnp.where(lane == group * STAT_LANES + place, value, stats)
    high = stats.astype(jnp.bfloat16).astype(jnp.float32)
    rest = stats - high
    middle = rest.astype(jnp.bfloat16).astype(jnp.float32)
    low = rest - middle
    pieces = high + pltpu.roll(middle, STATS, 1) + pltpu.roll(low, 2 * STATS, 1)
    filler = jnp.zeros((2 * HEAD_DIM - tokens, HEAD_DIM), jnp.float32)
    rows = jnp.concatenate([pieces, filler], axis=0).T
    packed = []
    for group in range(len(columns)):
        own = rows[group * STAT_LANES : (group + 1) * STAT_LANES]
        both = jnp.concatenate([own[:, :HEAD_DIM], own[:, HEAD_DIM:]], axis=0)
        packed.append(both.astype(jnp.bfloat16))
    return packed


def unpack_stats(packed, tokens):
    groups = packed.shape[0]
    rows = packed.astype(jnp.float32)
    filler = jnp.zeros((HEAD_DIM - groups * STAT_LANES, HEAD_DIM), jnp.float32)
    halves = [
        jnp.concatenate(
            [rows[group, half : half + STAT_LANES] for group in range(groups)] + [filler], axis=0
        )
        for half in (0, STAT_LANES)
    ]
    pieces = jnp.concatenate([half.T for half in halves], axis=0)[:tokens]
    return (
        pieces
        + pltpu.roll(pieces, HEAD_DIM - STATS, 1)
        + pltpu.roll(pieces, HEAD_DIM - 2 * STATS, 1)
    )


def split_kernel(local_ref, query_ref, key_value_ref, block_ref, semaphores):
    slots = local_ref.shape[0]
    rows = local_ref.shape[1] // 3
    for place in range(2):
        block = local_ref[:, pl.ds((place + 1) * rows, rows)]
        block_ref[place] = block.reshape(slots * rows, HEAD_DIM)
    copies = []
    for copy in range(key_value_ref.shape[0]):
        copies.append(
            pltpu.make_async_copy(block_ref, key_value_ref.at[copy], semaphores.at[copy])
        )
        copies[copy].start()
    query_ref[...] = local_ref[:, pl.ds(0, rows)].reshape(slots * rows, HEAD_DIM)
    for copy in copies:
        copy.wait()


def attend_kernel(q_ref, key_value_ref, out_ref):
    groups, tokens, width = q_ref.shape
    blocks = key_value_ref.shape[0] // KEY_BLOCKS
    count = blocks * tokens
    columns = []
    for group in range(0, groups, GROUP_STEP):
        query = q_ref[pl.ds(group, GROUP_STEP)].reshape(GROUP_STEP * tokens, width)
        scores = []
        for block in range(KEY_BLOCKS):
            key = key_value_ref[pl.ds(block * blocks, blocks), 0].reshape(count, width)
            scores.append(
                lax.dot_general(
                    query, key, (((1,), (1,)), ((), ())), preferred_element_type=jnp.float32
                )
            )
        highest = functools.reduce(
            jnp.maximum, [jnp.max(score, axis=1, keepdims=True) for score in scores]
        )
        total, summed = 0.0, 0.0
        for block, score in enumerate(scores):
            value = key_value_ref[pl.ds(block * blocks, blocks), 1].reshape(count, width)
            expd = jnp.exp2((score - highest) * (SCALE * LOG2E))
            total += jnp.sum(expd, axis=1, keepdims=True)
            summed += jnp.dot(expd.astype(jnp.bfloat16), value, preferred_element_type=jnp.float32)
        for step in range(GROUP_STEP):
            rows = slice(step * tokens, (step + 1) * tokens)
            out_ref[group + step, pl.ds(0, tokens)] = summed[rows].astype(jnp.bfloat16)
            columns.append((highest[rows], total[rows]))
    for group, packed in enumerate(pack_stats(columns)):
        out_ref[group, pl.ds(tokens, STAT_ROWS)] = packed


def combine_kernel(part_ref, out_ref):
    groups = part_ref.shape[0]
    tokens = part_ref.shape[1] - STAT_ROWS
    copies, rows, _ = out_ref.shape
    stats = unpack_stats(part_ref[:, pl.ds(tokens, STAT_ROWS)], tokens)
    lane = lax.broadcasted_iota(jnp.int32, stats.shape, 1)
    is_maximum = (lane % STAT_LANES == 0) & (lane < groups * STAT_LANES)
    highest = jnp.max(jnp.where(is_maximum, stats, -jnp.inf), axis=1, keepdims=True)
    weight = jnp.where(is_maximum, jnp.exp2((stats - highest) * (SCALE * LOG2E)), 0.0)
    sums = jnp.where(is_maximum, pltpu.roll(stats, HEAD_DIM - 1, 1), 0.0)
    total = jnp.sum(weight * sums, axis=1, keepdims=True)
    summed = jnp.zeros(stats.shape, jnp.float32)
    for group in range(groups):
        at = group * STAT_LANES
        part = part_ref[group, pl.ds(0, tokens)].astype(jnp.float32)
        summed += part * weight[:, at : at + 1]
    attended = (summed / total).astype(jnp.bfloat16)
    repeats = copies * rows // tokens
    for block in range(tokens // rows):
        for repeat in range(repeats):
            out_ref[block * repeats + repeat] = attended[block * rows : (block + 1) * rows]


def load_rows(weight_ref, held_ref, semaphores, first):
    rows = held_ref.shape[0] // semaphores.shape[0]
    copies = []
    for piece in range(semaphores.shape[0]):
        copy = pltpu.make_async_copy(
            weight_ref.at[pl.ds(first + piece * rows, rows)],
            held_ref.at[pl.ds(piece * rows, rows)],
            semaphores.at[piece],
        )
        copy.start()
        copies.append(copy)
    return copies


def fetch_kernel(weight_ref, gate_ref, held_ref, row_ref, semaphores):
    copies = load_rows(weight_ref, held_ref, semaphores, 0)
    row_ref[...] = gate_ref[...][None, :]
    for copy in copies:
        copy.wait()


def mix_kernel(attended_ref, row_ref, first_ref, weight_ref, out_ref, held_ref, semaphores):
    early = first_ref.shape[0] // HEAD_DIM
    copies = load_rows(weight_ref, held_ref, semaphores, first_ref.shape[0])
    span = held_ref.shape[0] // HEAD_DIM // len(copies)

    def product_of(first, count, rows):
        block = jnp.concatenate(
            [attended_ref[head] for head in range(first, first + count)], axis=1
        )
        return jnp.dot(block, rows, preferred_element_type=jnp.float32)

    product = product_of(0, early, first_ref[...])
    for piece, copy in enumerate(copies):
        copy.wait()
        rows = held_ref[pl.ds(piece * span * HEAD_DIM, span * HEAD_DIM)]
        product += product_of(early + piece * span, span, rows)
    out_ref[...] = (product * row_ref[...]).astype(jnp.bfloat16)


def exchange(blocks, axes):
    return lax.all_to_all(blocks, axes, split_axis=0, concat_axis=0, tiled=True)


def on_device(queries, keys, vals, out_weight, gate):
    slots = lax.axis_size(HEAD_AXES)
    rows, width = queries.shape
    heads = width // HEAD_DIM
    tokens = slots * rows
    own_tokens = lax.axis_size("tp") * rows
    stacked = jnp.stack([queries, keys, vals], axis=0).reshape(3, rows, heads, HEAD_DIM)
    stacked = stacked.transpose(2, 0, 1, 3).reshape(heads, 3 * rows, HEAD_DIM)
    stacked = jnp.pad(stacked, ((0, slots - heads), (0, 0), (0, 0)))
    own_query, key_value_copies = pl.pallas_call(
        split_kernel,
        out_shape=[
            jax.ShapeDtypeStruct((tokens, HEAD_DIM), jnp.bfloat16),
            jax.ShapeDtypeStruct((lax.axis_size(KEY_AXES), 2, tokens, HEAD_DIM), jnp.bfloat16),
        ],
        in_specs=[IN_VMEM],
        out_specs=[IN_VMEM, pl.BlockSpec(memory_space=pltpu.HBM)],
        scratch_shapes=[
            pltpu.VMEM((2, tokens, HEAD_DIM), jnp.bfloat16),
            pltpu.SemaphoreType.DMA((lax.axis_size(KEY_AXES),)),
        ],
        compiler_params=pltpu.CompilerParams(vmem_limit_bytes=KERNEL_VMEM),
        name="split",
    )(exchange(stacked, HEAD_AXES))
    channels = out_weight.shape[1]
    key_value_copies, weight = lax.optimization_barrier((key_value_copies, out_weight))
    in_hbm = pl.BlockSpec(memory_space=pltpu.HBM)
    first, row = pl.pallas_call(
        fetch_kernel,
        out_shape=[
            jax.ShapeDtypeStruct((EARLY_HEADS * HEAD_DIM, channels), weight.dtype),
            jax.ShapeDtypeStruct((1, channels), gate.dtype),
        ],
        in_specs=[in_hbm, IN_VMEM],
        out_specs=[IN_VMEM] * 2,
        scratch_shapes=[pltpu.SemaphoreType.DMA((EARLY_HEADS,))],
        compiler_params=pltpu.CompilerParams(vmem_limit_bytes=MIX_VMEM),
        cost_estimate=pl.CostEstimate(
            flops=0, bytes_accessed=4 * EARLY_HEADS * HEAD_DIM * channels, transcendentals=0
        ),
        name="fetch",
    )(weight, gate)
    key_value = exchange(key_value_copies, KEY_AXES)
    group = lax.all_gather(own_query, QUERY_AXES, axis=0, tiled=False)
    key_value, group, first, row = lax.optimization_barrier((key_value, group, first, row))
    partial = pl.pallas_call(
        attend_kernel,
        out_shape=jax.ShapeDtypeStruct(
            (group.shape[0], tokens + STAT_ROWS, HEAD_DIM), jnp.bfloat16
        ),
        in_specs=[IN_VMEM] * 2,
        out_specs=IN_VMEM,
        compiler_params=pltpu.CompilerParams(vmem_limit_bytes=KERNEL_VMEM),
        name="attend",
    )(group, key_value)
    partial = exchange(partial, QUERY_AXES)
    attended = pl.pallas_call(
        combine_kernel,
        out_shape=jax.ShapeDtypeStruct((slots, own_tokens, HEAD_DIM), jnp.bfloat16),
        in_specs=[IN_VMEM],
        out_specs=IN_VMEM,
        compiler_params=pltpu.CompilerParams(vmem_limit_bytes=KERNEL_VMEM),
        name="combine",
    )(partial)
    attended = exchange(attended, HEAD_AXES)
    late = heads - EARLY_HEADS
    return pl.pallas_call(
        mix_kernel,
        out_shape=jax.ShapeDtypeStruct((own_tokens, channels), jnp.bfloat16),
        in_specs=[IN_VMEM, IN_VMEM, IN_VMEM, in_hbm],
        out_specs=IN_VMEM,
        scratch_shapes=[
            pltpu.VMEM((late * HEAD_DIM, channels), out_weight.dtype),
            pltpu.SemaphoreType.DMA((late,)),
        ],
        compiler_params=pltpu.CompilerParams(vmem_limit_bytes=MIX_VMEM),
        name="mix",
    )(attended, row, first, weight)


def solution(mesh):
    ctx = ("zl", "y", "x", "c")
    fine = Mesh(mesh.devices.reshape(3, 8, 4, 2, 4), (*ctx, "tp"))
    return jax.shard_map(
        on_device,
        mesh=fine,
        in_specs=(
            P((*ctx, "tp"), None),
            P((*ctx, "tp"), None),
            P((*ctx, "tp"), None),
            P(None, "tp"),
            P("tp"),
        ),
        out_specs=P(ctx, "tp"),
        check_vma=False,
    )
```

```python
import functools

import jax
import jax.numpy as jnp
from jax import lax
from jax.experimental import pallas as pl
from jax.experimental.pallas import tpu as pltpu
from jax.sharding import Mesh, PartitionSpec as P

HEAD_DIM = 128
LOG2E = 1.4426950408889634
SCALE = HEAD_DIM ** -0.5
HEAD_AXES = ("zl", "c", "tp")
QUERY_AXES = ("x",)
KEY_AXES = ("y",)
STATS = 2
STAT_LANES = 8
STAT_ROWS = 16
GROUP_STEP = 2
KEY_BLOCKS = 4
EARLY_HEADS = 6
KERNEL_VMEM = 16 * 1024 * 1024
MIX_VMEM = 50 * 1024 * 1024
IN_VMEM = pl.BlockSpec(memory_space=pltpu.VMEM)


def pack_stats(columns):
    tokens = columns[0][0].shape[0]
    lane = lax.broadcasted_iota(jnp.int32, (tokens, HEAD_DIM), 1)
    stats = jnp.zeros((tokens, HEAD_DIM), jnp.float32)
    for group, values in enumerate(columns):
        for place, value in enumerate(values):
            stats = jnp.where(lane == group * STAT_LANES + place, value, stats)
    high = stats.astype(jnp.bfloat16).astype(jnp.float32)
    rest = stats - high
    middle = rest.astype(jnp.bfloat16).astype(jnp.float32)
    low = rest - middle
    pieces = high + pltpu.roll(middle, STATS, 1) + pltpu.roll(low, 2 * STATS, 1)
    filler = jnp.zeros((2 * HEAD_DIM - tokens, HEAD_DIM), jnp.float32)
    rows = jnp.concatenate([pieces, filler], axis=0).T
    packed = []
    for group in range(len(columns)):
        own = rows[group * STAT_LANES : (group + 1) * STAT_LANES]
        both = jnp.concatenate([own[:, :HEAD_DIM], own[:, HEAD_DIM:]], axis=0)
        packed.append(both.astype(jnp.bfloat16))
    return packed


def unpack_stats(packed, tokens):
    groups = packed.shape[0]
    rows = packed.astype(jnp.float32)
    filler = jnp.zeros((HEAD_DIM - groups * STAT_LANES, HEAD_DIM), jnp.float32)
    halves = [
        jnp.concatenate(
            [rows[group, half : half + STAT_LANES] for group in range(groups)] + [filler], axis=0
        )
        for half in (0, STAT_LANES)
    ]
    pieces = jnp.concatenate([half.T for half in halves], axis=0)[:tokens]
    return (
        pieces
        + pltpu.roll(pieces, HEAD_DIM - STATS, 1)
        + pltpu.roll(pieces, HEAD_DIM - 2 * STATS, 1)
    )


def split_kernel(local_ref, query_ref, key_value_ref, block_ref, semaphores):
    slots = local_ref.shape[0]
    rows = local_ref.shape[1] // 3
    for place in range(2):
        block = local_ref[:, pl.ds((place + 1) * rows, rows)]
        block_ref[place] = block.reshape(slots * rows, HEAD_DIM)
    copies = []
    for copy in range(key_value_ref.shape[0]):
        copies.append(
            pltpu.make_async_copy(block_ref, key_value_ref.at[copy], semaphores.at[copy])
        )
        copies[copy].start()
    query_ref[...] = local_ref[:, pl.ds(0, rows)].reshape(slots * rows, HEAD_DIM)
    for copy in copies:
        copy.wait()


def attend_kernel(q_ref, key_value_ref, out_ref):
    groups, tokens, width = q_ref.shape
    blocks = key_value_ref.shape[0] // KEY_BLOCKS
    count = blocks * tokens
    columns = []
    for group in range(0, groups, GROUP_STEP):
        query = q_ref[pl.ds(group, GROUP_STEP)].reshape(GROUP_STEP * tokens, width)
        scores = []
        for block in range(KEY_BLOCKS):
            key = key_value_ref[pl.ds(block * blocks, blocks), 0].reshape(count, width)
            scores.append(
                lax.dot_general(
                    query, key, (((1,), (1,)), ((), ())), preferred_element_type=jnp.float32
                )
            )
        highest = functools.reduce(
            jnp.maximum, [jnp.max(score, axis=1, keepdims=True) for score in scores]
        )
        total, summed = 0.0, 0.0
        for block, score in enumerate(scores):
            value = key_value_ref[pl.ds(block * blocks, blocks), 1].reshape(count, width)
            expd = jnp.exp2((score - highest) * (SCALE * LOG2E))
            total += jnp.sum(expd, axis=1, keepdims=True)
            summed += jnp.dot(expd.astype(jnp.bfloat16), value, preferred_element_type=jnp.float32)
        for step in range(GROUP_STEP):
            rows = slice(step * tokens, (step + 1) * tokens)
            out_ref[group + step, pl.ds(0, tokens)] = summed[rows].astype(jnp.bfloat16)
            columns.append((highest[rows], total[rows]))
    for group, packed in enumerate(pack_stats(columns)):
        out_ref[group, pl.ds(tokens, STAT_ROWS)] = packed


def combine_kernel(part_ref, out_ref):
    groups = part_ref.shape[0]
    tokens = part_ref.shape[1] - STAT_ROWS
    copies, rows, _ = out_ref.shape
    stats = unpack_stats(part_ref[:, pl.ds(tokens, STAT_ROWS)], tokens)
    lane = lax.broadcasted_iota(jnp.int32, stats.shape, 1)
    is_maximum = (lane % STAT_LANES == 0) & (lane < groups * STAT_LANES)
    highest = jnp.max(jnp.where(is_maximum, stats, -jnp.inf), axis=1, keepdims=True)
    weight = jnp.where(is_maximum, jnp.exp2((stats - highest) * (SCALE * LOG2E)), 0.0)
    sums = jnp.where(is_maximum, pltpu.roll(stats, HEAD_DIM - 1, 1), 0.0)
    total = jnp.sum(weight * sums, axis=1, keepdims=True)
    summed = jnp.zeros(stats.shape, jnp.float32)
    for group in range(groups):
        at = group * STAT_LANES
        part = part_ref[group, pl.ds(0, tokens)].astype(jnp.float32)
        summed += part * weight[:, at : at + 1]
    attended = (summed / total).astype(jnp.bfloat16)
    repeats = copies * rows // tokens
    for block in range(tokens // rows):
        for repeat in range(repeats):
            out_ref[block * repeats + repeat] = attended[block * rows : (block + 1) * rows]


def load_rows(weight_ref, held_ref, semaphores, first):
    rows = held_ref.shape[0] // semaphores.shape[0]
    copies = []
    for piece in range(semaphores.shape[0]):
        copy = pltpu.make_async_copy(
            weight_ref.at[pl.ds(first + piece * rows, rows)],
            held_ref.at[pl.ds(piece * rows, rows)],
            semaphores.at[piece],
        )
        copy.start()
        copies.append(copy)
    return copies


def fetch_kernel(weight_ref, gate_ref, held_ref, row_ref, semaphores):
    copies = load_rows(weight_ref, held_ref, semaphores, 0)
    row_ref[...] = gate_ref[...][None, :]
    for copy in copies:
        copy.wait()


def mix_kernel(attended_ref, row_ref, first_ref, weight_ref, out_ref, held_ref, semaphores):
    early = first_ref.shape[0] // HEAD_DIM
    copies = load_rows(weight_ref, held_ref, semaphores, first_ref.shape[0])
    span = held_ref.shape[0] // HEAD_DIM // len(copies)

    def product_of(first, count, rows):
        block = jnp.concatenate(
            [attended_ref[head] for head in range(first, first + count)], axis=1
        )
        return jnp.dot(block, rows, preferred_element_type=jnp.float32)

    product = product_of(0, early, first_ref[...])
    for piece, copy in enumerate(copies):
        copy.wait()
        rows = held_ref[pl.ds(piece * span * HEAD_DIM, span * HEAD_DIM)]
        product += product_of(early + piece * span, span, rows)
    out_ref[...] = (product * row_ref[...]).astype(jnp.bfloat16)


def exchange(blocks, axes):
    return lax.all_to_all(blocks, axes, split_axis=0, concat_axis=0, tiled=True)


def on_device(queries, keys, vals, out_weight, gate):
    slots = lax.axis_size(HEAD_AXES)
    rows, width = queries.shape
    heads = width // HEAD_DIM
    tokens = slots * rows
    own_tokens = lax.axis_size("tp") * rows
    stacked = jnp.stack([queries, keys, vals], axis=0).reshape(3, rows, heads, HEAD_DIM)
    stacked = stacked.transpose(2, 0, 1, 3).reshape(heads, 3 * rows, HEAD_DIM)
    stacked = jnp.pad(stacked, ((0, slots - heads), (0, 0), (0, 0)))
    own_query, key_value_copies = pl.pallas_call(
        split_kernel,
        out_shape=[
            jax.ShapeDtypeStruct((tokens, HEAD_DIM), jnp.bfloat16),
            jax.ShapeDtypeStruct((lax.axis_size(KEY_AXES), 2, tokens, HEAD_DIM), jnp.bfloat16),
        ],
        in_specs=[IN_VMEM],
        out_specs=[IN_VMEM, pl.BlockSpec(memory_space=pltpu.HBM)],
        scratch_shapes=[
            pltpu.VMEM((2, tokens, HEAD_DIM), jnp.bfloat16),
            pltpu.SemaphoreType.DMA((lax.axis_size(KEY_AXES),)),
        ],
        compiler_params=pltpu.CompilerParams(vmem_limit_bytes=KERNEL_VMEM),
        name="split",
    )(exchange(stacked, HEAD_AXES))
    channels = out_weight.shape[1]
    group = lax.all_gather(own_query, QUERY_AXES, axis=0, tiled=False)
    group, weight = lax.optimization_barrier((group, out_weight))
    in_hbm = pl.BlockSpec(memory_space=pltpu.HBM)
    first, row = pl.pallas_call(
        fetch_kernel,
        out_shape=[
            jax.ShapeDtypeStruct((EARLY_HEADS * HEAD_DIM, channels), weight.dtype),
            jax.ShapeDtypeStruct((1, channels), gate.dtype),
        ],
        in_specs=[in_hbm, IN_VMEM],
        out_specs=[IN_VMEM] * 2,
        scratch_shapes=[pltpu.SemaphoreType.DMA((EARLY_HEADS // 2,))],
        compiler_params=pltpu.CompilerParams(vmem_limit_bytes=MIX_VMEM),
        cost_estimate=pl.CostEstimate(
            flops=0, bytes_accessed=4 * EARLY_HEADS * HEAD_DIM * channels, transcendentals=0
        ),
        name="fetch",
    )(weight, gate)
    key_value = exchange(key_value_copies, KEY_AXES)
    key_value, group, first, row = lax.optimization_barrier((key_value, group, first, row))
    partial = pl.pallas_call(
        attend_kernel,
        out_shape=jax.ShapeDtypeStruct(
            (group.shape[0], tokens + STAT_ROWS, HEAD_DIM), jnp.bfloat16
        ),
        in_specs=[IN_VMEM] * 2,
        out_specs=IN_VMEM,
        compiler_params=pltpu.CompilerParams(vmem_limit_bytes=KERNEL_VMEM),
        name="attend",
    )(group, key_value)
    partial = exchange(partial, QUERY_AXES)
    attended = pl.pallas_call(
        combine_kernel,
        out_shape=jax.ShapeDtypeStruct((slots, own_tokens, HEAD_DIM), jnp.bfloat16),
        in_specs=[IN_VMEM],
        out_specs=IN_VMEM,
        compiler_params=pltpu.CompilerParams(vmem_limit_bytes=KERNEL_VMEM),
        name="combine",
    )(partial)
    attended = exchange(attended, HEAD_AXES)
    late = heads - EARLY_HEADS
    return pl.pallas_call(
        mix_kernel,
        out_shape=jax.ShapeDtypeStruct((own_tokens, channels), jnp.bfloat16),
        in_specs=[IN_VMEM, IN_VMEM, IN_VMEM, in_hbm],
        out_specs=IN_VMEM,
        scratch_shapes=[
            pltpu.VMEM((late * HEAD_DIM, channels), out_weight.dtype),
            pltpu.SemaphoreType.DMA((late // 2,)),
        ],
        compiler_params=pltpu.CompilerParams(vmem_limit_bytes=MIX_VMEM),
        name="mix",
    )(attended, row, first, weight)


def solution(mesh):
    ctx = ("zl", "y", "x", "c")
    fine = Mesh(mesh.devices.reshape(3, 8, 4, 2, 4), (*ctx, "tp"))
    return jax.shard_map(
        on_device,
        mesh=fine,
        in_specs=(
            P((*ctx, "tp"), None),
            P((*ctx, "tp"), None),
            P((*ctx, "tp"), None),
            P(None, "tp"),
            P("tp"),
        ),
        out_specs=P(ctx, "tp"),
        check_vma=False,
    )
```
